32 devices in a mesh: dp: 4 (over x, core), ctx: 8 (over z, y).
Axes of the slice: x: 2, y: 2, z: 4, core: 2. Of those that a mesh axis runs over, the one named last changes fastest.
Arguments:
- queries: bfloat16 [4, 1024, 1024], P('dp', 'ctx'), may hold values from -60 to 60
- keys: bfloat16 [4, 1024, 128], P('dp', 'ctx'), may hold values from -6 to 6
- values: bfloat16 [4, 1024, 192], P('dp', 'ctx'), may hold values from -96 to 96
- features_fine: bfloat16 [4, 2048, 1536], P('dp', 'ctx'), may hold values from -6 to 6
- rc_state: bfloat16 [4, 1024, 1536], P('dp', 'ctx'), may hold values from -6 to 6
- conv_weight: float32 [5, 1536], replicated, may hold values from -2.5 to 2.5
Outputs:
- d_fine: bfloat16 [4, 2048, 1536], P('dp', 'ctx')
- d_weight: float32 [5, 1536], replicated
The draws below stay inside these ranges and needn't reach their ends.
All inputs are finite; a program needn't handle non-finite values.
Results may differ from the reference program's by a relative error of at most 0.0085.
Values may be sent and summed in bfloat16 or wider, within the bound.
No kernel may reach another device: no remote copies, remote signals or barrier semaphores. Data moves between devices by JAX's collectives and lax.ppermute only.
A program may use at most 64 MiB of HBM per device.

```python
import math
import jax
import jax.numpy as jnp
from jax import lax

D = 1536
HEADS = 8
DK = 128
DV = 192
KW = 5
LEN = 1024
XLEN = 2048
SEQS = 4


def shared_keys(key):
    sub = jax.random.fold_in(key, 11)
    base = jnp.clip(jax.random.normal(sub, (SEQS, LEN, DK), jnp.float32), -6.0, 6.0)
    return base


def draw_keys(key, part):
    return shared_keys(key).astype(jnp.bfloat16)


def draw_queries(key, part):
    sub = jax.random.fold_in(key, 12)
    out = jnp.clip(jax.random.normal(sub, (SEQS, LEN, HEADS, DK), jnp.float32), -6.0, 6.0)
    return out.reshape(SEQS, LEN, HEADS * DK).astype(jnp.bfloat16)


def shard_levels(rng, dims, pieces, low, top_value):
    gain = 1.0
    for axis_at, blocks in pieces:
        heights = jax.random.uniform(jax.random.fold_in(jax.random.fold_in(rng, 6), axis_at), (blocks,), jnp.float32, low / len(pieces), top_value / len(pieces))
        gain = gain * jnp.repeat(jnp.exp(heights), dims[axis_at] // blocks).reshape((-1,) + (1,) * (len(dims) - 1 - axis_at))
    return gain


def bell_draw(stream_key, shape, spread, limit, shards=(), held_as=jnp.bfloat16):
    drawn = jax.random.normal(stream_key, shape, jnp.float32) * spread
    if len(shards) > 0:
        drawn = shard_levels(stream_key, shape, shards, -0.22, 0.18) * drawn
    return jnp.clip(drawn, min=-limit, max=limit).astype(held_as)


def setup_inputs(seed: int = 0) -> dict:
    key_of = jax.random.split(jax.random.key(seed), 7)
    return {
        "queries": draw_queries(jax.random.fold_in(key_of[6], 71), 0),
        "keys": draw_keys(jax.random.fold_in(key_of[6], 71), 0),
        "values": bell_draw(key_of[2], (SEQS, LEN, DV), 16.0, 96.0, ((0, 4), (1, 8))),
        "features_fine": bell_draw(key_of[3], (SEQS, XLEN, D), 1.0, 6.0, ((0, 4), (1, 8))),
        "rc_state": bell_draw(key_of[4], (SEQS, LEN, D), 1.0, 6.0, ((0, 4), (1, 8))),
        "conv_weight": bell_draw(key_of[5], (KW, D), KW ** -0.5, 2.5, (), jnp.float32),
    }


def attend_block(block, keys_f, values_f):
    rows = block.shape[0]
    q_f = block.astype(jnp.float32).reshape(rows, HEADS, DK)
    scores = jnp.einsum('qhd,kd->qhk', q_f, keys_f) * DK ** (-0.5)
    top = lax.optimization_barrier(jnp.max(scores, axis=-1, keepdims=True))
    expd = jnp.exp(scores - top)
    total = lax.optimization_barrier(jnp.sum(expd, axis=-1))
    weights = expd.astype(jnp.bfloat16).astype(jnp.float32)
    out = jnp.einsum('qhk,kv->qhv', weights, values_f) / total[..., None]
    return out.reshape(rows, HEADS * DV)

def attend_seq(items):
    q_seq, k_seq, v_seq = items
    keys_f = k_seq.astype(jnp.float32)
    values_f = v_seq.astype(jnp.float32)
    block = math.gcd(LEN, 512)
    blocks = q_seq.reshape(LEN // block, block, HEADS * DK)
    out = lax.map(lambda b: attend_block(b, keys_f, values_f), blocks)
    return out.reshape(LEN, HEADS * DV)

def reference(queries, keys, values, features_fine, rc_state, conv_weight):
    attended = lax.map(attend_seq, (queries, keys, values))
    fine = features_fine.astype(jnp.float32)
    padded = jnp.pad(fine, ((0, 0), (2, 2), (0, 0)))
    taps = [padded[:, k:k + 2 * LEN:2, :] for k in range(KW)]
    coarse = jnp.zeros((SEQS, LEN, D), jnp.float32)
    for k in range(KW):
        coarse = coarse + conv_weight[k] * taps[k]
    grad = coarse + attended - rc_state[:, ::-1, :].astype(jnp.float32)
    gpad = jnp.pad(grad, ((0, 0), (1, 1), (0, 0)))
    even = conv_weight[0] * gpad[:, 2:] + conv_weight[2] * gpad[:, 1:-1] + conv_weight[4] * gpad[:, :-2]
    odd = conv_weight[1] * gpad[:, 2:] + conv_weight[3] * gpad[:, 1:-1]
    d_fine = jnp.stack([even, odd], axis=2).reshape(SEQS, XLEN, D).astype(jnp.bfloat16)
    scale = 1.0 / math.sqrt(SEQS * LEN)
    d_weight = jnp.stack([lax.optimization_barrier(jnp.sum(grad * taps[k], axis=(0, 1))) for k in range(KW)]) * scale
    return (d_fine, d_weight)
```

```python
import math

import jax
import jax.numpy as jnp
from jax import lax
from jax.experimental import pallas as pl
from jax.experimental.pallas import tpu as pltpu
from jax.sharding import PartitionSpec as P

HEADS = 8
KW = 5
EDGE = 8
LANES = 128


def attend_kernel(edge, q, up, down, f, w, *rest, blocks):
    kv = rest[:blocks]
    base, base_edge, fine, keys, vals_lo, vals_hi, att = rest[blocks:]
    rows = q.shape[0]
    dk = q.shape[1] // HEADS
    per = kv[0].shape[1]
    dv = kv[0].shape[0] - per
    wide = vals_lo.shape[0]
    up_f = up[...].astype(jnp.float32)
    down_f = down[...].astype(jnp.float32)
    for c in range(fine.shape[0]):
        at = slice(c * LANES, (c + 1) * LANES)
        fine[c, 0:EDGE] = up_f[:, at]
        fine[c, EDGE : EDGE + 2 * rows] = f[:, at].astype(jnp.float32)
        fine[c, EDGE + 2 * rows :] = down_f[:, at]
    for j in range(blocks):
        keys[j * per : (j + 1) * per] = kv[j][0:per]
        vals_lo[0:dv, j * per : (j + 1) * per] = kv[j][per:]
        vals_hi[wide - dv :, j * per : (j + 1) * per] = kv[j][per:]
    vals_lo[dv:] = jnp.zeros((wide - dv, blocks * per), vals_lo.dtype)
    vals_hi[0 : wide - dv] = jnp.zeros((wide - dv, blocks * per), vals_hi.dtype)
    q_edge = jnp.concatenate(
        [up_f[1:2, : HEADS * dk], down_f[5:6, : HEADS * dk], jnp.zeros((14, HEADS * dk), jnp.float32)], axis=0
    ).astype(q.dtype)
    scale = dk ** (-0.5)

    def head(h, vals):
        q_h = jnp.concatenate([q[:, h * dk : (h + 1) * dk], q_edge[:, h * dk : (h + 1) * dk]], axis=0)
        s = lax.dot_general(q_h, keys[...], (((1,), (1,)), ((), ())), preferred_element_type=jnp.float32) * scale
        p = jnp.exp(s - jnp.max(s, axis=1, keepdims=True))
        total = jnp.sum(p, axis=1, keepdims=True)
        o = lax.dot_general(
            p.astype(jnp.bfloat16), vals[...], (((1,), (1,)), ((), ())), preferred_element_type=jnp.float32
        )
        return o / total

    for pair in range(HEADS // 2):
        lo = head(2 * pair, vals_lo)
        hi = head(2 * pair + 1, vals_hi)
        at = 2 * dv * pair
        over = 2 * wide - 2 * dv
        att[:, at : at + wide - over] = lo[:, : wide - over]
        att[:, at + wide - over : at + wide] = lo[:, wide - over :] + hi[:, :over]
        att[:, at + wide : at + 2 * dv] = hi[:, over:]
    first = edge[0] == 0
    last = edge[0] == edge[1] - 1
    for c in range(fine.shape[0]):
        at = slice(c * LANES, (c + 1) * LANES)
        acc = att[0:rows, at]
        left = att[rows : rows + 1, at]
        right = att[rows + 1 : rows + 2, at]
        for k in range(KW):
            w_k = w[k : k + 1, at]
            acc = acc + w_k * fine[c, pl.ds(EDGE - 2 + k, rows, stride=2), :]
            left = left + w_k * fine[c, EDGE - 4 + k : EDGE - 3 + k]
            right = right + w_k * fine[c, EDGE + 2 * rows - 2 + k : EDGE + 2 * rows - 1 + k]
        base[:, at] = acc
        base_edge[0:1, at] = jnp.where(first, 0.0, left)
        base_edge[1:2, at] = jnp.where(last, 0.0, right)


def grad_kernel(base, base_edge, fine, rc, rc_edge, partial, grad):
    rows = base.shape[0]
    flip = (
        lax.broadcasted_iota(jnp.int32, (rows, rows), 0) + lax.broadcasted_iota(jnp.int32, (rows, rows), 1) == rows - 1
    ).astype(jnp.bfloat16)
    for c in range(fine.shape[0]):
        at = slice(c * LANES, (c + 1) * LANES)
        g = base[:, at] - jnp.dot(flip, rc[:, at], preferred_element_type=jnp.float32)
        ends = base_edge[0:2, at] - rc_edge[:, at].astype(jnp.float32)
        grad[EDGE : EDGE + rows, at] = g
        grad[EDGE - 1 : EDGE, at] = ends[0:1]
        grad[EDGE + rows : EDGE + rows + 1, at] = ends[1:2]
        for k in range(KW):
            partial[k : k + 1, at] = jnp.sum(
                g * fine[c, pl.ds(EDGE - 2 + k, rows, stride=2), :], axis=0, keepdims=True
            )


def fine_kernel(grad, w, d_fine, wide):
    rows = d_fine.shape[0] // 2
    for c in range(wide.shape[0]):
        at = slice(c * LANES, (c + 1) * LANES)
        here = grad[EDGE : EDGE + rows, at]
        after = grad[EDGE + 1 : EDGE + 1 + rows, at]
        before = grad[EDGE - 1 : EDGE - 1 + rows, at]
        wide[c, pl.ds(0, rows, stride=2), :] = w[0:1, at] * after + w[2:3, at] * here + w[4:5, at] * before
        wide[c, pl.ds(1, rows, stride=2), :] = w[1:2, at] * after + w[3:4, at] * here
        d_fine[:, at] = wide[c].astype(d_fine.dtype)


def swap(value, axis, mask):
    return lax.ppermute(value, axis, [(i, i ^ mask) for i in range(lax.axis_size(axis))])


def body(queries, keys, values, features_fine, rc_state, conv_weight):
    count = lax.axis_size("ctx")
    q, f, rc = queries[0], features_fine[0], rc_state[0]
    rows, chans = rc.shape
    qw = q.shape[1]
    here = lax.axis_index("ctx")
    edge = jnp.stack([here, jnp.full_like(here, count)]).astype(jnp.int32)

    own = jnp.concatenate([keys[0], values[0].T], axis=0)
    if count <= 8:
        got = [own] + [swap(own, "ctx", m) for m in range(2, count, 2)]
        blocks = got + [swap(b, "ctx", 1) for b in got]
    else:
        gathered = lax.all_gather(own, "ctx")
        blocks = [gathered[i] for i in range(count)]

    q_pad = ((0, 0), (0, chans - qw))
    zero = jnp.zeros((2, chans), rc.dtype)
    to_up = jnp.concatenate([rc[-1:], jnp.pad(q[-1:], q_pad), zero, f[-4:]], axis=0)
    to_down = jnp.concatenate([f[:4], rc[:1], jnp.pad(q[:1], q_pad), zero], axis=0)
    up = lax.ppermute(to_up, "ctx", [(i, i + 1) for i in range(count - 1)])
    down = lax.ppermute(to_down, "ctx", [(i + 1, i) for i in range(count - 1)])
    across = [(i, count - 1 - i) for i in range(count)]
    mirrored = lax.ppermute(rc, "ctx", across)
    mirrored_edge = lax.ppermute(jnp.concatenate([down[4:5], up[0:1]], axis=0), "ctx", across)

    n = len(blocks)
    dv = values.shape[2]
    wide = pl.cdiv(dv, 128) * 128
    vmem = pl.BlockSpec(memory_space=pltpu.VMEM)
    base, base_edge, fine = pl.pallas_call(
        lambda *refs: attend_kernel(*refs, blocks=n),
        name="attend",
        out_shape=(
            jax.ShapeDtypeStruct((rows, chans), jnp.float32),
            jax.ShapeDtypeStruct((EDGE, chans), jnp.float32),
            jax.ShapeDtypeStruct((chans // LANES, 2 * rows + 2 * EDGE, LANES), jnp.float32),
        ),
        in_specs=[pl.BlockSpec(memory_space=pltpu.SMEM)] + [vmem] * (5 + n),
        out_specs=(vmem, vmem, vmem),
        scratch_shapes=[
            pltpu.VMEM((n * rows, keys.shape[2]), jnp.bfloat16),
            pltpu.VMEM((wide, n * rows), jnp.bfloat16),
            pltpu.VMEM((wide, n * rows), jnp.bfloat16),
            pltpu.VMEM((rows + 16, chans), jnp.float32),
        ],
    )(edge, q, up, down, f, conv_weight, *blocks)

    partial, grad = pl.pallas_call(
        grad_kernel,
        name="grad",
        out_shape=(
            jax.ShapeDtypeStruct((KW, chans), jnp.float32),
            jax.ShapeDtypeStruct((rows + 2 * EDGE, chans), jnp.float32),
        ),
        in_specs=[vmem] * 5,
        out_specs=(vmem, vmem),
    )(base, base_edge, fine, mirrored, mirrored_edge)

    d_fine = pl.pallas_call(
        fine_kernel,
        name="fine",
        out_shape=jax.ShapeDtypeStruct((2 * rows, chans), jnp.bfloat16),
        in_specs=[vmem] * 2,
        out_specs=vmem,
        scratch_shapes=[pltpu.VMEM((chans // LANES, 2 * rows, LANES), jnp.float32)],
    )(grad, conv_weight)

    total = partial
    for axis in ("dp", "ctx"):
        mask = 1
        while mask < lax.axis_size(axis):
            total = total + swap(total, axis, mask)
            mask *= 2
    scale = 1.0 / math.sqrt(lax.axis_size("dp") * rows * count)
    return (d_fine[None], total * scale)


def solution(mesh):
    placed = (
        P("dp", "ctx", None),
        P("dp", "ctx", None),
        P("dp", "ctx", None),
        P("dp", "ctx", None),
        P("dp", "ctx", None),
        P(),
    )
    return jax.shard_map(
        body, mesh=mesh, in_specs=placed, out_specs=(P("dp", "ctx", None), P()), check_vma=False
    )
```

```python
import math

import jax
import jax.numpy as jnp
from jax import lax
from jax.experimental import pallas as pl
from jax.experimental.pallas import tpu as pltpu
from jax.sharding import PartitionSpec as P


HEADS = 8
KW = 5
EDGE = 8
LANES = 128


def attend_kernel(edge, q, up, down, f, w, *rest, blocks):
    kv = rest[:blocks]
    base, base_edge, fine, keys, vals_lo, vals_hi, att = rest[blocks:]
    rows = q.shape[0]
    dk = q.shape[1] // HEADS
    per = kv[0].shape[1]
    dv = kv[0].shape[0] - per
    wide = vals_lo.shape[0]
    up_f = up[...].astype(jnp.float32)
    down_f = down[...].astype(jnp.float32)
    for c in range(fine.shape[0]):
        at = slice(c * LANES, (c + 1) * LANES)
        fine[c, 0:EDGE] = up_f[:, at]
        fine[c, EDGE : EDGE + 2 * rows] = f[:, at].astype(jnp.float32)
        fine[c, EDGE + 2 * rows :] = down_f[:, at]
    for j in range(blocks):
        keys[j * per : (j + 1) * per] = kv[j][0:per]
        vals_lo[0:dv, j * per : (j + 1) * per] = kv[j][per:]
        vals_hi[wide - dv :, j * per : (j + 1) * per] = kv[j][per:]
    vals_lo[dv:] = jnp.zeros((wide - dv, blocks * per), vals_lo.dtype)
    vals_hi[0 : wide - dv] = jnp.zeros((wide - dv, blocks * per), vals_hi.dtype)
    q_edge = jnp.concatenate(
        [up_f[1:2, : HEADS * dk], down_f[5:6, : HEADS * dk], jnp.zeros((14, HEADS * dk), jnp.float32)], axis=0
    ).astype(q.dtype)
    scale = dk ** (-0.5)

    def head(h, vals):
        q_h = jnp.concatenate([q[:, h * dk : (h + 1) * dk], q_edge[:, h * dk : (h + 1) * dk]], axis=0)
        s = lax.dot_general(q_h, keys[...], (((1,), (1,)), ((), ())), preferred_element_type=jnp.float32) * scale
        p = jnp.exp(s - jnp.max(s, axis=1, keepdims=True))
        total = jnp.sum(p, axis=1, keepdims=True)
        o = lax.dot_general(
            p.astype(jnp.bfloat16), vals[...], (((1,), (1,)), ((), ())), preferred_element_type=jnp.float32
        )
        return o / total

    for pair in range(HEADS // 2):
        lo = head(2 * pair, vals_lo)
        hi = head(2 * pair + 1, vals_hi)
        at = 2 * dv * pair
        over = 2 * wide - 2 * dv
        att[:, at : at + wide - over] = lo[:, : wide - over]
        att[:, at + wide - over : at + wide] = lo[:, wide - over :] + hi[:, :over]
        att[:, at + wide : at + 2 * dv] = hi[:, over:]
    first = edge[0] == 0
    last = edge[0] == edge[1] - 1
    for c in range(fine.shape[0]):
        at = slice(c * LANES, (c + 1) * LANES)
        acc = att[0:rows, at]
        left = att[rows : rows + 1, at]
        right = att[rows + 1 : rows + 2, at]
        for k in range(KW):
            w_k = w[k : k + 1, at]
            acc = acc + w_k * fine[c, pl.ds(EDGE - 2 + k, rows, stride=2), :]
            left = left + w_k * fine[c, EDGE - 4 + k : EDGE - 3 + k]
            right = right + w_k * fine[c, EDGE + 2 * rows - 2 + k : EDGE + 2 * rows - 1 + k]
        base[:, at] = acc
        base_edge[0:1, at] = jnp.where(first, 0.0, left)
        base_edge[1:2, at] = jnp.where(last, 0.0, right)


def grad_kernel(base, fine, rc_a, rc_b, partial, grad):
    rows = base.shape[0]
    half = rows // 2
    flip = (
        lax.broadcasted_iota(jnp.int32, (half, half), 0) + lax.broadcasted_iota(jnp.int32, (half, half), 1) == half - 1
    ).astype(jnp.bfloat16)
    for c in range(fine.shape[0]):
        at = slice(c * LANES, (c + 1) * LANES)
        sums = [None] * KW
        for low, rc in ((half, rc_a), (0, rc_b)):
            g = base[low : low + half, at] - jnp.dot(flip, rc[:, at], preferred_element_type=jnp.float32)
            grad[low : low + half, at] = g
            for k in range(KW):
                tap = fine[c, pl.ds(EDGE - 2 + k + 2 * low, half, stride=2), :]
                term = jnp.sum((g * tap).reshape(half // 8, 8, LANES), axis=0)
                sums[k] = term if sums[k] is None else sums[k] + term
        for k in range(KW):
            partial[k : k + 1, at] = jnp.sum(sums[k], axis=0, keepdims=True)


def fine_kernel(grad, base_edge, rc_edge, w, d_fine, wide, padded):
    rows = d_fine.shape[0] // 2
    for c in range(wide.shape[0]):
        at = slice(c * LANES, (c + 1) * LANES)
        here = grad[:, at]
        ends = base_edge[0:2, at] - rc_edge[:, at].astype(jnp.float32)
        padded[EDGE : EDGE + rows] = here
        padded[EDGE - 1 : EDGE] = ends[0:1]
        padded[EDGE + rows : EDGE + rows + 1] = ends[1:2]
        after = padded[EDGE + 1 : EDGE + 1 + rows]
        before = padded[EDGE - 1 : EDGE - 1 + rows]
        wide[c, pl.ds(0, rows, stride=2), :] = w[0:1, at] * after + w[2:3, at] * here + w[4:5, at] * before
        wide[c, pl.ds(1, rows, stride=2), :] = w[1:2, at] * after + w[3:4, at] * here
        d_fine[:, at] = wide[c].astype(d_fine.dtype)


def swap(value, axis, mask):
    return lax.ppermute(value, axis, [(i, i ^ mask) for i in range(lax.axis_size(axis))])


def near(value):
    return pltpu.with_memory_space_constraint(value, pltpu.VMEM)


def body(queries, keys, values, features_fine, rc_state, conv_weight):
    count = lax.axis_size("ctx")
    q, f, rc = queries[0], features_fine[0], rc_state[0]
    rows, chans = rc.shape
    qw = q.shape[1]
    here = lax.axis_index("ctx")
    edge = jnp.stack([here, jnp.full_like(here, count)]).astype(jnp.int32)

    own = jnp.concatenate([keys[0], values[0].T], axis=0)
    half = rows // 2
    if count == 8:
        k6 = swap(own, "ctx", 6)
        k2 = swap(own, "ctx", 2)
        k1 = swap(own, "ctx", 1)
        k62 = swap(k6, "ctx", 2)
        k61 = swap(k6, "ctx", 1)
        k21 = swap(k2, "ctx", 1)
        k621 = swap(k62, "ctx", 1)
        blocks = [own, k6, k2, k1, k62, k61, k21, k621]
        rc_a = swap(swap(rc[:half], "ctx", 6), "ctx", 1)
        rc_b = swap(swap(rc[half:], "ctx", 1), "ctx", 6)
    else:
        gathered = lax.all_gather(own, "ctx")
        blocks = [gathered[i] for i in range(count)]
        rc_a = swap(rc[:half], "ctx", count - 1)
        rc_b = swap(rc[half:], "ctx", count - 1)

    q_pad = ((0, 0), (0, chans - qw))
    zero = jnp.zeros((2, chans), rc.dtype)
    to_up = jnp.concatenate([rc[-1:], jnp.pad(q[-1:], q_pad), zero, f[-4:]], axis=0)
    to_down = jnp.concatenate([f[:4], rc[:1], jnp.pad(q[:1], q_pad), zero], axis=0)
    up = lax.ppermute(to_up, "ctx", [(i, i + 1) for i in range(count - 1)])
    down = lax.ppermute(to_down, "ctx", [(i + 1, i) for i in range(count - 1)])
    rc_edge = swap(jnp.concatenate([down[4:5], up[0:1]], axis=0), "ctx", count - 1)

    n = len(blocks)
    dv = values.shape[2]
    wide = pl.cdiv(dv, 128) * 128
    vmem = pl.BlockSpec(memory_space=pltpu.VMEM)
    base, base_edge, fine = pl.pallas_call(
        lambda *refs: attend_kernel(*refs, blocks=n),
        name="attend",
        out_shape=(
            pltpu.VMEM((rows, chans), jnp.float32),
            pltpu.VMEM((EDGE, chans), jnp.float32),
            pltpu.VMEM((chans // LANES, 2 * rows + 2 * EDGE, LANES), jnp.float32),
        ),
        in_specs=[pl.BlockSpec(memory_space=pltpu.SMEM)] + [vmem] * (5 + n),
        out_specs=(vmem, vmem, vmem),
        scratch_shapes=[
            pltpu.VMEM((n * rows, keys.shape[2]), jnp.bfloat16),
            pltpu.VMEM((wide, n * rows), jnp.bfloat16),
            pltpu.VMEM((wide, n * rows), jnp.bfloat16),
            pltpu.VMEM((rows + 16, chans), jnp.float32),
        ],
        compiler_params=pltpu.CompilerParams(vmem_limit_bytes=24 << 20),
    )(edge, q, near(up), near(down), f, conv_weight, *[near(b) for b in blocks])

    partial, grad = pl.pallas_call(
        grad_kernel,
        name="grad",
        out_shape=(pltpu.VMEM((KW, chans), jnp.float32), pltpu.VMEM((rows, chans), jnp.float32)),
        in_specs=[vmem] * 4,
        out_specs=(vmem, vmem),
        compiler_params=pltpu.CompilerParams(vmem_limit_bytes=8 << 20),
    )(near(base), near(fine), near(rc_a), near(rc_b))

    d_fine = pl.pallas_call(
        fine_kernel,
        name="fine",
        out_shape=jax.ShapeDtypeStruct((2 * rows, chans), jnp.bfloat16),
        in_specs=[vmem] * 4,
        out_specs=vmem,
        scratch_shapes=[
            pltpu.VMEM((chans // LANES, 2 * rows, LANES), jnp.float32),
            pltpu.VMEM((rows + 2 * EDGE, LANES), jnp.float32),
        ],
        compiler_params=pltpu.CompilerParams(vmem_limit_bytes=8 << 20),
    )(near(grad), near(base_edge), near(rc_edge), conv_weight)

    total = partial
    for axis in ("dp", "ctx"):
        mask = 1
        while mask < lax.axis_size(axis):
            total = total + swap(total, axis, mask)
            mask *= 2
    scale = 1.0 / math.sqrt(lax.axis_size("dp") * rows * count)
    return (d_fine[None], total * scale)


def solution(mesh):
    placed = (
        P("dp", "ctx", None),
        P("dp", "ctx", None),
        P("dp", "ctx", None),
        P("dp", "ctx", None),
        P("dp", "ctx", None),
        P(),
    )

    return jax.shard_map(body, mesh=mesh, in_specs=placed, out_specs=(P("dp", "ctx", None), P()), check_vma=False)
```

```python
import math

import jax
import jax.numpy as jnp
from jax import lax
from jax.experimental import pallas as pl
from jax.experimental.pallas import tpu as pltpu
from jax.sharding import PartitionSpec as P


HEADS = 8
KW = 5
EDGE = 8
LANES = 128
TAIL = 4
HEAD = 3
TILE = 16
CUT = 2
VMEM = pl.BlockSpec(memory_space=pltpu.VMEM)
HBM = pl.BlockSpec(memory_space=pltpu.HBM)
SMEM = pl.BlockSpec(memory_space=pltpu.SMEM)


def edge_rows(tiles, heads):
    at = {}
    start = 0
    for name, count in (
        ("f_tail", TAIL * tiles),
        ("f_head", HEAD * tiles),
        ("rc_first", tiles),
        ("rc_last", tiles),
        ("q_first", heads),
        ("q_last", heads),
    ):
        at[name] = start
        start += count
    return at, pl.cdiv(start, TILE) * TILE


def pack_kernel(k, vt, q, f, rc, own, rc_a, rc_b, q_ends, f_ends, rc_ends, edges, sem):
    dk, dv = k.shape[0], vt.shape[0]
    half = rc_a.shape[0]
    q_rows, f_rows, rc_rows = q.shape[0], f.shape[0], rc.shape[0]
    copies = [
        (rc.at[0:TILE], rc_ends.at[0:TILE]),
        (rc.at[rc_rows - TILE :], rc_ends.at[TILE:]),
        (q.at[0:TILE], q_ends.at[0:TILE]),
        (q.at[q_rows - TILE :], q_ends.at[TILE:]),
        (f.at[0:TILE], f_ends.at[0:TILE]),
        (f.at[f_rows - TILE :], f_ends.at[TILE:]),
        (k, own.at[0:dk]),
        (vt, own.at[dk : dk + dv]),
        (rc.at[0:half], rc_a),
        (rc.at[half:], rc_b),
    ]
    started = [pltpu.make_async_copy(src, dst, sem.at[i]) for i, (src, dst) in enumerate(copies)]
    for copy in started:
        copy.start()
    for copy in started[:6]:
        copy.wait()
    tiles = rc.shape[1] // LANES
    heads = q.shape[1] // LANES
    at, _ = edge_rows(tiles, heads)
    rc_f = rc_ends[...].astype(jnp.float32)
    q_f = q_ends[...].astype(jnp.float32)
    f_f = f_ends[...].astype(jnp.float32)
    edges[...] = jnp.zeros(edges.shape, jnp.float32)
    for c in range(tiles):
        to = slice(c * LANES, (c + 1) * LANES)
        for j in range(TAIL):
            edges[at["f_tail"] + j * tiles + c] = f_f[2 * TILE - TAIL + j, to]
        for j in range(HEAD):
            edges[at["f_head"] + j * tiles + c] = f_f[j, to]
        edges[at["rc_first"] + c] = rc_f[0, to]
        edges[at["rc_last"] + c] = rc_f[2 * TILE - 1, to]
    for h in range(heads):
        to = slice(h * LANES, (h + 1) * LANES)
        edges[at["q_first"] + h] = q_f[0, to]
        edges[at["q_last"] + h] = q_f[2 * TILE - 1, to]
    own[dk + dv :] = edges[...].astype(own.dtype)
    for copy in started[6:]:
        copy.wait()


def prep_kernel(q, f, w, q_near, w_near, coarse, fine, f_near, sem):
    started = [
        pltpu.make_async_copy(f, f_near, sem.at[0]),
        pltpu.make_async_copy(w, w_near, sem.at[1]),
        pltpu.make_async_copy(q, q_near, sem.at[2]),
    ]
    for copy in started:
        copy.start()
    for copy in started:
        copy.wait()
    rows = coarse.shape[0]
    for c in range(fine.shape[0]):
        to = slice(c * LANES, (c + 1) * LANES)
        fine[c, 0:EDGE] = jnp.zeros((EDGE, LANES), jnp.float32)
        fine[c, EDGE : EDGE + 2 * rows] = f_near[:, to].astype(jnp.float32)
        fine[c, EDGE + 2 * rows :] = jnp.zeros((EDGE, LANES), jnp.float32)
        acc = w_near[0:1, to] * fine[c, pl.ds(EDGE - 2, rows, stride=2), :]
        for k in range(1, KW):
            acc = acc + w_near[k : k + 1, to] * fine[c, pl.ds(EDGE - 2 + k, rows, stride=2), :]
        coarse[:, to] = acc


def attend_kernel(place, q, w, coarse, fine_in, *rest, parts, per, dv):
    kv = rest[:parts]
    base, ends, fine, keys, vals_lo, vals_hi, edges, att_ends = rest[parts:]
    rows, chans = coarse.shape
    dk = q.shape[1] // HEADS
    wide = vals_lo.shape[0]
    blocks = edges.shape[0]
    tiles = chans // LANES
    at, count = edge_rows(tiles, HEADS)
    j = 0
    for part in kv:
        for low in range(0, part.shape[0], per + dv + count):
            keys[j * per : (j + 1) * per] = part[low : low + per]
            vals_lo[0:dv, j * per : (j + 1) * per] = part[low + per : low + per + dv]
            vals_hi[wide - dv :, j * per : (j + 1) * per] = part[low + per : low + per + dv]
            edges[j] = part[low + per + dv : low + per + dv + count].astype(jnp.float32)
            j += 1
    vals_lo[dv:] = jnp.zeros((wide - dv, blocks * per), vals_lo.dtype)
    vals_hi[0 : wide - dv] = jnp.zeros((wide - dv, blocks * per), vals_hi.dtype)
    has_left = place[0]
    has_right = place[1]
    left_at = place[2]
    right_at = place[3]
    scale = dk ** (-0.5)

    def head(h, vals):
        q_h = jnp.concatenate(
            [
                q[:, h * dk : (h + 1) * dk].astype(jnp.float32),
                edges[left_at, at["q_last"] + h : at["q_last"] + h + 1],
                edges[right_at, at["q_first"] + h : at["q_first"] + h + 1],
                jnp.zeros((TILE - 2, dk), jnp.float32),
            ],
            axis=0,
        ).astype(q.dtype)
        s = lax.dot_general(q_h, keys[...], (((1,), (1,)), ((), ())), preferred_element_type=jnp.float32) * scale
        p = jnp.exp(s - jnp.max(s, axis=1, keepdims=True))
        total = jnp.sum(p, axis=1, keepdims=True)
        o = lax.dot_general(
            p.astype(jnp.bfloat16), vals[...], (((1,), (1,)), ((), ())), preferred_element_type=jnp.float32
        )
        return o / total

    over = 2 * wide - 2 * dv
    for pair in range(HEADS // 2):
        lo = head(2 * pair, vals_lo)
        hi = head(2 * pair + 1, vals_hi)
        first = 2 * dv * pair
        pieces = (
            (first, lo[:, : wide - over]),
            (first + wide - over, lo[:, wide - over :] + hi[:, :over]),
            (first + wide, hi[:, over:]),
        )
        for start, piece in pieces:
            to = slice(start, start + piece.shape[1])
            base[:, to] = coarse[:, to] + piece[:rows]
            att_ends[:, to] = piece[rows : rows + EDGE]
    keep_left = has_left == 1
    keep_right = has_right == 1
    rc_left_at = place[4]
    rc_right_at = place[5]
    last = 2 * rows + EDGE
    for c in range(tiles):
        to = slice(c * LANES, (c + 1) * LANES)
        for i in range(TAIL):
            row = at["f_tail"] + i * tiles + c
            fine[c, EDGE - TAIL + i : EDGE - TAIL + i + 1] = jnp.where(keep_left, edges[left_at, row : row + 1], 0.0)
        for i in range(HEAD):
            row = at["f_head"] + i * tiles + c
            fine[c, last + i : last + i + 1] = jnp.where(keep_right, edges[right_at, row : row + 1], 0.0)
        w_c = [w[k : k + 1, to] for k in range(KW)]
        base[0:1, to] = base[0:1, to] + w_c[0] * fine[c, EDGE - 2 : EDGE - 1] + w_c[1] * fine[c, EDGE - 1 : EDGE]
        base[rows - 1 : rows, to] = base[rows - 1 : rows, to] + w_c[4] * fine[c, last : last + 1]
        row = at["rc_first"] + c
        left = att_ends[0:1, to] - edges[rc_left_at, row : row + 1]
        row = at["rc_last"] + c
        right = att_ends[1:2, to] - edges[rc_right_at, row : row + 1]
        for k in range(KW):
            left = left + w_c[k] * fine[c, EDGE - 4 + k : EDGE - 3 + k]
            right = right + w_c[k] * fine[c, last - 2 + k : last - 1 + k]
        ends[0:1, to] = jnp.where(keep_left, left, 0.0)
        ends[1:2, to] = jnp.where(keep_right, right, 0.0)


def grad_kernel(base, fine, rc_a, rc_b, partial, grad):
    rows = base.shape[0]

    def flip(n):
        i = lax.broadcasted_iota(jnp.int32, (n, n), 0)
        j = lax.broadcasted_iota(jnp.int32, (n, n), 1)
        return (i + j == n - 1).astype(jnp.bfloat16)

    pieces = [(rows - rc_a.shape[0], rc_a, flip(rc_a.shape[0])), (0, rc_b, flip(rc_b.shape[0]))]
    for c in range(fine.shape[0]):
        to = slice(c * LANES, (c + 1) * LANES)
        sums = [None] * KW
        for low, rc, turn in pieces:
            n = rc.shape[0]
            g = base[low : low + n, to] - jnp.dot(turn, rc[:, to], preferred_element_type=jnp.float32)
            grad[low : low + n, to] = g
            for k in range(KW):
                tap = fine[c, pl.ds(EDGE - 2 + k + 2 * low, n, stride=2), :]
                term = jnp.sum((g * tap).reshape(n // 8, 8, LANES), axis=0)
                sums[k] = term if sums[k] is None else sums[k] + term
        for k in range(KW):
            partial[k : k + 1, to] = jnp.sum(sums[k], axis=0, keepdims=True)


def fine_kernel(grad, ends, w, d_fine, wide, padded):
    rows = d_fine.shape[0] // 2
    for c in range(wide.shape[0]):
        to = slice(c * LANES, (c + 1) * LANES)
        here = grad[:, to]
        padded[EDGE : EDGE + rows] = here
        padded[EDGE - 1 : EDGE] = ends[0:1, to]
        padded[EDGE + rows : EDGE + rows + 1] = ends[1:2, to]
        after = padded[EDGE + 1 : EDGE + 1 + rows]
        before = padded[EDGE - 1 : EDGE - 1 + rows]
        wide[c, pl.ds(0, rows, stride=2), :] = w[0:1, to] * after + w[2:3, to] * here + w[4:5, to] * before
        wide[c, pl.ds(1, rows, stride=2), :] = w[1:2, to] * after + w[3:4, to] * here
        d_fine[:, to] = wide[c].astype(d_fine.dtype)


def swap(value, axis, mask):
    return lax.ppermute(value, axis, [(i, i ^ mask) for i in range(lax.axis_size(axis))])


def near(value):
    return pltpu.with_memory_space_constraint(value, pltpu.VMEM)


def far(value):
    return pltpu.with_memory_space_constraint(value, pltpu.HBM)


def limit(mib):
    return pltpu.CompilerParams(vmem_limit_bytes=mib << 20)


def body(queries, keys, values, features_fine, rc_state, conv_weight):
    count = lax.axis_size("ctx")
    q, f, rc = queries[0], features_fine[0], rc_state[0]
    rows, chans = rc.shape
    tiles = chans // LANES
    cut = rows * CUT // 8
    dk, dv = keys.shape[2], values.shape[2]
    _, extra = edge_rows(tiles, HEADS)
    size = rows + dv + extra
    bf16, f32 = jnp.bfloat16, jnp.float32

    own, rc_a, rc_b = pl.pallas_call(
        pack_kernel,
        name="pack",
        out_shape=(pltpu.VMEM((size, LANES), bf16), pltpu.VMEM((cut, chans), bf16), pltpu.VMEM((rows - cut, chans), bf16)),
        in_specs=[HBM] * 5,
        out_specs=(VMEM, VMEM, VMEM),
        scratch_shapes=[
            pltpu.VMEM((2 * TILE, q.shape[1]), bf16),
            pltpu.VMEM((2 * TILE, chans), bf16),
            pltpu.VMEM((2 * TILE, chans), bf16),
            pltpu.VMEM((extra, LANES), f32),
            pltpu.SemaphoreType.DMA((10,)),
        ],
        compiler_params=limit(4),
    )(far(keys[0]), far(values[0].T), far(q), far(f), far(rc))

    here = lax.axis_index("ctx").astype(jnp.int32)
    wanted = jnp.stack([here - 1, here + 1, count - here, count - 2 - here])
    if count == 8:
        k4 = swap(own, "ctx", 4)
        rc_b = swap(rc_b, "ctx", 1)
        pair = jnp.concatenate([own, k4], axis=0)
        k2 = swap(pair, "ctx", 2)
        k1 = swap(pair, "ctx", 1)
        rc_a = swap(rc_a, "ctx", 6)
        rc_b = swap(rc_b, "ctx", 6)
        k21 = swap(k2, "ctx", 1)
        rc_a = swap(rc_a, "ctx", 1)
        parts = [pair, k2, k1, k21]
        mask = here ^ wanted
        wanted = ((mask & 1) * 4) | (mask & 2) | ((mask & 4) // 4)
    else:
        parts = [lax.all_gather(own, "ctx", axis=0, tiled=True)]
        rc_a = swap(rc_a, "ctx", count - 1)
        rc_b = swap(rc_b, "ctx", count - 1)
    wanted = jnp.clip(wanted, 0, count - 1)
    ends_of = jnp.stack([here > 0, here < count - 1]).astype(jnp.int32)
    place = jnp.concatenate([ends_of, wanted])

    q_near, w_near, coarse, fine = pl.pallas_call(
        prep_kernel,
        name="prep",
        out_shape=(
            pltpu.VMEM(q.shape, bf16),
            pltpu.VMEM(conv_weight.shape, f32),
            pltpu.VMEM((rows, chans), f32),
            pltpu.VMEM((tiles, 2 * rows + 2 * EDGE, LANES), f32),
        ),
        in_specs=[HBM] * 3,
        out_specs=(VMEM,) * 4,
        scratch_shapes=[pltpu.VMEM(f.shape, bf16), pltpu.SemaphoreType.DMA((3,))],
        compiler_params=limit(8),
    )(far(q), far(f), far(conv_weight))

    wide = pl.cdiv(dv, LANES) * LANES
    base, ends, fine = pl.pallas_call(
        lambda *refs: attend_kernel(*refs, parts=len(parts), per=rows, dv=dv),
        name="attend",
        out_shape=(
            pltpu.VMEM((rows, chans), f32),
            pltpu.VMEM((EDGE, chans), f32),
            pltpu.VMEM((tiles, 2 * rows + 2 * EDGE, LANES), f32),
        ),
        in_specs=[SMEM] + [VMEM] * (4 + len(parts)),
        out_specs=(VMEM,) * 3,
        scratch_shapes=[
            pltpu.VMEM((count * rows, dk), bf16),
            pltpu.VMEM((wide, count * rows), bf16),
            pltpu.VMEM((wide, count * rows), bf16),
            pltpu.VMEM((count, extra, LANES), f32),
            pltpu.VMEM((EDGE, chans), f32),
        ],
        input_output_aliases={3: 0, 4: 2},
        compiler_params=limit(24),
    )(place, near(q_near), near(w_near), near(coarse), near(fine), *[near(part) for part in parts])

    partial, grad = pl.pallas_call(
        grad_kernel,
        name="grad",
        out_shape=(pltpu.VMEM((KW, chans), f32), pltpu.VMEM((rows, chans), f32)),
        in_specs=[VMEM] * 4,
        out_specs=(VMEM,) * 2,
        compiler_params=limit(8),
    )(near(base), near(fine), near(rc_a), near(rc_b))

    d_fine = pl.pallas_call(
        fine_kernel,
        name="fine",
        out_shape=jax.ShapeDtypeStruct((2 * rows, chans), bf16),
        in_specs=[VMEM] * 3,
        out_specs=VMEM,
        scratch_shapes=[
            pltpu.VMEM((tiles, 2 * rows, LANES), f32),
            pltpu.VMEM((rows + 2 * EDGE, LANES), f32),
        ],
        compiler_params=limit(8),
    )(near(grad), near(ends), near(w_near))

    total = partial
    if count == 8:
        rounds = [("dp", (1 << b,)) for b in range(lax.axis_size("dp").bit_length() - 1)]
        rounds += [("ctx", (1, 2, 3)), ("ctx", (4,))]
    else:
        rounds = [(a, (1 << b,)) for a in ("dp", "ctx") for b in range(lax.axis_size(a).bit_length() - 1)]
    for axis, masks in rounds:
        got = [swap(total, axis, mask) for mask in masks]
        total = sum(got, total)
    scale = 1.0 / math.sqrt(lax.axis_size("dp") * rows * count)
    return (d_fine[None], total * scale)


def solution(mesh):
    placed = (
        P("dp", "ctx", None),
        P("dp", "ctx", None),
        P("dp", "ctx", None),
        P("dp", "ctx", None),
        P("dp", "ctx", None),
        P(),
    )

    return jax.shard_map(body, mesh=mesh, in_specs=placed, out_specs=(P("dp", "ctx", None), P()), check_vma=False)
```

```python
import math

import jax
import jax.numpy as jnp
from jax import lax
from jax.experimental import pallas as pl
from jax.experimental.pallas import tpu as pltpu
from jax.sharding import PartitionSpec as P


HEADS = 8
KW = 5
EDGE = 8
LANES = 128
TAIL = 4
HEAD = 3
TILE = 16
CUT = 3
VMEM = pl.BlockSpec(memory_space=pltpu.VMEM)
HBM = pl.BlockSpec(memory_space=pltpu.HBM)
SMEM = pl.BlockSpec(memory_space=pltpu.SMEM)


def edge_rows(tiles, heads):
    at = {}
    start = 0
    for name, count in (
        ("f_tail", TAIL * tiles),
        ("f_head", HEAD * tiles),
        ("rc_first", tiles),
        ("rc_last", tiles),
        ("q_first", heads),
        ("q_last", heads),
    ):
        at[name] = start
        start += count
    return at, pl.cdiv(start, TILE) * TILE


def pack_kernel(k, vt, q, f, rc, own, rc_a, rc_b, q_ends, f_ends, rc_ends, edges, sem):
    dk, dv = k.shape[0], vt.shape[0]
    half = rc_a.shape[0]
    q_rows, f_rows, rc_rows = q.shape[0], f.shape[0], rc.shape[0]
    copies = [
        (rc.at[0:TILE], rc_ends.at[0:TILE]),
        (rc.at[rc_rows - TILE :], rc_ends.at[TILE:]),
        (q.at[0:TILE], q_ends.at[0:TILE]),
        (q.at[q_rows - TILE :], q_ends.at[TILE:]),
        (f.at[0:TILE], f_ends.at[0:TILE]),
        (f.at[f_rows - TILE :], f_ends.at[TILE:]),
        (k, own.at[0:dk]),
        (vt, own.at[dk : dk + dv]),
        (rc.at[0:half], rc_a),
        (rc.at[half:], rc_b),
    ]
    started = [pltpu.make_async_copy(src, dst, sem.at[i]) for i, (src, dst) in enumerate(copies)]
    for copy in started:
        copy.start()
    for copy in started[:6]:
        copy.wait()
    tiles = rc.shape[1] // LANES
    heads = q.shape[1] // LANES
    at, _ = edge_rows(tiles, heads)
    rc_f = rc_ends[...].astype(jnp.float32)
    q_f = q_ends[...].astype(jnp.float32)
    f_f = f_ends[...].astype(jnp.float32)
    edges[...] = jnp.zeros(edges.shape, jnp.float32)
    for c in range(tiles):
        to = slice(c * LANES, (c + 1) * LANES)
        for j in range(TAIL):
            edges[at["f_tail"] + j * tiles + c] = f_f[2 * TILE - TAIL + j, to]
        for j in range(HEAD):
            edges[at["f_head"] + j * tiles + c] = f_f[j, to]
        edges[at["rc_first"] + c] = rc_f[0, to]
        edges[at["rc_last"] + c] = rc_f[2 * TILE - 1, to]
    for h in range(heads):
        to = slice(h * LANES, (h + 1) * LANES)
        edges[at["q_first"] + h] = q_f[0, to]
        edges[at["q_last"] + h] = q_f[2 * TILE - 1, to]
    own[dk + dv :] = edges[...].astype(own.dtype)
    for copy in started[6:]:
        copy.wait()


def prep_kernel(q, f, w, q_near, w_near, coarse, fine, f_near, sem):
    started = [
        pltpu.make_async_copy(f, f_near, sem.at[0]),
        pltpu.make_async_copy(w, w_near, sem.at[1]),
        pltpu.make_async_copy(q, q_near, sem.at[2]),
    ]
    for copy in started:
        copy.start()
    for copy in started:
        copy.wait()
    rows = coarse.shape[0]
    for c in range(fine.shape[0]):
        to = slice(c * LANES, (c + 1) * LANES)
        fine[c, 0:EDGE] = jnp.zeros((EDGE, LANES), jnp.float32)
        fine[c, EDGE : EDGE + 2 * rows] = f_near[:, to].astype(jnp.float32)
        fine[c, EDGE + 2 * rows :] = jnp.zeros((EDGE, LANES), jnp.float32)
        acc = w_near[0:1, to] * fine[c, pl.ds(EDGE - 2, rows, stride=2), :]
        for k in range(1, KW):
            acc = acc + w_near[k : k + 1, to] * fine[c, pl.ds(EDGE - 2 + k, rows, stride=2), :]
        coarse[:, to] = acc


def load_blocks(blocks, per, dv, keys, vals_lo, vals_hi):
    wide = vals_lo.shape[0]
    for j, (ref, low) in enumerate(blocks):
        to = slice(j * per, (j + 1) * per)
        keys[to] = ref[low : low + per]
        vals_lo[0:dv, to] = ref[low + per : low + per + dv]
        vals_hi[wide - dv :, to] = ref[low + per : low + per + dv]
    span = len(blocks) * per
    vals_lo[dv:] = jnp.zeros((wide - dv, span), vals_lo.dtype)
    vals_hi[0 : wide - dv] = jnp.zeros((wide - dv, span), vals_hi.dtype)


def times(a, b):
    return lax.dot_general(a, b, (((1,), (1,)), ((), ())), preferred_element_type=jnp.float32)


def first_kernel(q, *rest, parts, per, dv, count):
    refs = rest[:parts]
    keys, vals_lo, vals_hi, tops, totals, sums = rest[parts:]
    dk = q.shape[1] // HEADS
    blocks = block_list(refs, per + dv + count)
    load_blocks(blocks[: keys.shape[0] // per], per, dv, keys, vals_lo, vals_hi)
    scale = dk ** (-0.5)
    for h in range(HEADS):
        vals = vals_hi if h % 2 else vals_lo
        s = times(q[:, h * dk : (h + 1) * dk], keys[...]) * scale
        top = jnp.max(s, axis=1, keepdims=True)
        p = jnp.exp(s - top)
        tops[h] = jnp.broadcast_to(top, tops.shape[1:])
        totals[h] = jnp.broadcast_to(jnp.sum(p, axis=1, keepdims=True), totals.shape[1:])
        sums[h] = times(p.astype(jnp.bfloat16), vals[...])


def block_list(refs, size):
    return [(ref, low) for ref in refs for low in range(0, ref.shape[0], size)]


def attend_kernel(q, w, coarse, fine_in, keys_a, lo_a, hi_a, tops, totals, sums, *rest, parts, per, dv, ring):
    refs = rest[:parts]
    base, ends, fine, keys, vals_lo, vals_hi, edges, att_ends = rest[parts:]
    rows, chans = coarse.shape
    dk = q.shape[1] // HEADS
    wide = vals_lo.shape[0]
    tiles = chans // LANES
    at, count = edge_rows(tiles, HEADS)
    blocks = block_list(refs, per + dv + count)
    total_blocks = len(blocks)
    load_blocks(blocks[total_blocks // 2 :], per, dv, keys, vals_lo, vals_hi)
    for j, (ref, low) in enumerate(blocks):
        edges[j] = ref[low + per + dv : low + per + dv + count].astype(jnp.float32)
    here = lax.axis_index("ctx").astype(jnp.int32)

    def spot(other):
        if not ring:
            return jnp.clip(other, 0, total_blocks - 1)
        mask = (here ^ other) & (total_blocks - 1)
        return ((mask & 1) * 4) | (mask & 2) | ((mask & 4) // 4)

    keep_left = here > 0
    keep_right = here < total_blocks - 1
    left_at, right_at = spot(here - 1), spot(here + 1)
    rc_left_at, rc_right_at = spot(total_blocks - here), spot(total_blocks - 2 - here)
    scale = dk ** (-0.5)
    over = 2 * wide - 2 * dv

    def head(h):
        vals = vals_hi if h % 2 else vals_lo
        s = times(q[:, h * dk : (h + 1) * dk], keys[...]) * scale
        old = tops[h, :, 0:1]
        top = jnp.maximum(old, jnp.max(s, axis=1, keepdims=True))
        fade = jnp.exp(old - top)
        p = jnp.exp(s - top)
        total = totals[h, :, 0:1] * fade + jnp.sum(p, axis=1, keepdims=True)
        return (sums[h] * fade + times(p.astype(jnp.bfloat16), vals[...])) / total

    def spread(h, lo, hi):
        start = dv * h
        return (
            (start, lo[:, : wide - over]),
            (start + wide - over, lo[:, wide - over :] + hi[:, :over]),
            (start + wide, hi[:, over:]),
        )

    for h in range(0, HEADS, 2):
        for start, piece in spread(h, head(h), head(h + 1)):
            to = slice(start, start + piece.shape[1])
            base[:, to] = coarse[:, to] + piece

    q_edge = jnp.concatenate(
        [
            edges[left_at, at["q_last"] : at["q_last"] + HEADS],
            edges[right_at, at["q_first"] : at["q_first"] + HEADS],
        ],
        axis=0,
    ).astype(q.dtype)
    s_a = times(q_edge, keys_a[...]) * scale
    s_b = times(q_edge, keys[...]) * scale
    top = jnp.maximum(jnp.max(s_a, axis=1, keepdims=True), jnp.max(s_b, axis=1, keepdims=True))
    p_a, p_b = jnp.exp(s_a - top), jnp.exp(s_b - top)
    total = jnp.sum(p_a, axis=1, keepdims=True) + jnp.sum(p_b, axis=1, keepdims=True)
    p_a, p_b = p_a.astype(jnp.bfloat16), p_b.astype(jnp.bfloat16)
    edge_lo = (times(p_a, lo_a[...]) + times(p_b, vals_lo[...])) / total
    edge_hi = (times(p_a, hi_a[...]) + times(p_b, vals_hi[...])) / total
    for side in range(2):
        for h in range(0, HEADS, 2):
            i = side * HEADS + h
            for start, piece in spread(h, edge_lo[i : i + 1], edge_hi[i + 1 : i + 2]):
                att_ends[side : side + 1, start : start + piece.shape[1]] = piece

    last = 2 * rows + EDGE
    for c in range(tiles):
        to = slice(c * LANES, (c + 1) * LANES)
        for i in range(TAIL):
            row = at["f_tail"] + i * tiles + c
            fine[c, EDGE - TAIL + i : EDGE - TAIL + i + 1] = jnp.where(keep_left, edges[left_at, row : row + 1], 0.0)
        for i in range(HEAD):
            row = at["f_head"] + i * tiles + c
            fine[c, last + i : last + i + 1] = jnp.where(keep_right, edges[right_at, row : row + 1], 0.0)
        w_c = [w[k : k + 1, to] for k in range(KW)]
        base[0:1, to] = base[0:1, to] + w_c[0] * fine[c, EDGE - 2 : EDGE - 1] + w_c[1] * fine[c, EDGE - 1 : EDGE]
        base[rows - 1 : rows, to] = base[rows - 1 : rows, to] + w_c[4] * fine[c, last : last + 1]
        row = at["rc_first"] + c
        left = att_ends[0:1, to] - edges[rc_left_at, row : row + 1]
        row = at["rc_last"] + c
        right = att_ends[1:2, to] - edges[rc_right_at, row : row + 1]
        for k in range(KW):
            left = left + w_c[k] * fine[c, EDGE - 4 + k : EDGE - 3 + k]
            right = right + w_c[k] * fine[c, last - 2 + k : last - 1 + k]
        ends[0:1, to] = jnp.where(keep_left, left, 0.0)
        ends[1:2, to] = jnp.where(keep_right, right, 0.0)


def grad_kernel(base, fine, rc_a, rc_b, partial, grad):
    rows = base.shape[0]

    def flip(n):
        i = lax.broadcasted_iota(jnp.int32, (n, n), 0)
        j = lax.broadcasted_iota(jnp.int32, (n, n), 1)
        return (i + j == n - 1).astype(jnp.bfloat16)

    pieces = [(rows - rc_a.shape[0], rc_a, flip(rc_a.shape[0])), (0, rc_b, flip(rc_b.shape[0]))]
    for c in range(fine.shape[0]):
        to = slice(c * LANES, (c + 1) * LANES)
        sums = [None] * KW
        for low, rc, turn in pieces:
            n = rc.shape[0]
            g = base[low : low + n, to] - jnp.dot(turn, rc[:, to], preferred_element_type=jnp.float32)
            grad[low : low + n, to] = g
            for k in range(KW):
                tap = fine[c, pl.ds(EDGE - 2 + k + 2 * low, n, stride=2), :]
                term = jnp.sum((g * tap).reshape(n // 8, 8, LANES), axis=0)
                sums[k] = term if sums[k] is None else sums[k] + term
        for k in range(KW):
            partial[k : k + 1, to] = jnp.sum(sums[k], axis=0, keepdims=True)


def fine_kernel(grad, ends, w, d_fine, wide, padded):
    rows = d_fine.shape[0] // 2
    for c in range(wide.shape[0]):
        to = slice(c * LANES, (c + 1) * LANES)
        here = grad[:, to]
        padded[EDGE : EDGE + rows] = here
        padded[EDGE - 1 : EDGE] = ends[0:1, to]
        padded[EDGE + rows : EDGE + rows + 1] = ends[1:2, to]
        after = padded[EDGE + 1 : EDGE + 1 + rows]
        before = padded[EDGE - 1 : EDGE - 1 + rows]
        wide[c, pl.ds(0, rows, stride=2), :] = w[0:1, to] * after + w[2:3, to] * here + w[4:5, to] * before
        wide[c, pl.ds(1, rows, stride=2), :] = w[1:2, to] * after + w[3:4, to] * here
        d_fine[:, to] = wide[c].astype(d_fine.dtype)


def swap(value, axis, mask):
    return lax.ppermute(value, axis, [(i, i ^ mask) for i in range(lax.axis_size(axis))])


def near(value):
    return pltpu.with_memory_space_constraint(value, pltpu.VMEM)


def far(value):
    return pltpu.with_memory_space_constraint(value, pltpu.HBM)


def limit(mib):
    return pltpu.CompilerParams(vmem_limit_bytes=mib << 20)


def body(queries, keys, values, features_fine, rc_state, conv_weight):
    count = lax.axis_size("ctx")
    q, f, rc = queries[0], features_fine[0], rc_state[0]
    rows, chans = rc.shape
    tiles = chans // LANES
    cut = rows * CUT // 8
    dk, dv = keys.shape[2], values.shape[2]
    _, extra = edge_rows(tiles, HEADS)
    size = rows + dv + extra
    bf16, f32 = jnp.bfloat16, jnp.float32

    own, rc_a, rc_b = pl.pallas_call(
        pack_kernel,
        name="pack",
        out_shape=(pltpu.VMEM((size, LANES), bf16), pltpu.VMEM((cut, chans), bf16), pltpu.VMEM((rows - cut, chans), bf16)),
        in_specs=[HBM] * 5,
        out_specs=(VMEM, VMEM, VMEM),
        scratch_shapes=[
            pltpu.VMEM((2 * TILE, q.shape[1]), bf16),
            pltpu.VMEM((2 * TILE, chans), bf16),
            pltpu.VMEM((2 * TILE, chans), bf16),
            pltpu.VMEM((extra, LANES), f32),
            pltpu.SemaphoreType.DMA((10,)),
        ],
        compiler_params=limit(4),
    )(far(keys[0]), far(values[0].T), far(q), far(f), far(rc))

    if count == 8:
        k4 = swap(own, "ctx", 4)
        k2a = swap(own, "ctx", 2)
        k1a = swap(own, "ctx", 1)
        rc_b = swap(rc_b, "ctx", 1)
        rc_a = swap(rc_a, "ctx", 6)
        k2b = swap(k4, "ctx", 2)
        k21a = swap(k2a, "ctx", 1)
        k1b = swap(k4, "ctx", 1)
        rc_b = swap(rc_b, "ctx", 6)
        k21b = swap(k2b, "ctx", 1)
        rc_a = swap(rc_a, "ctx", 1)
        early = [own, k4, k2a, k2b]
        parts = early + [k1a, k1b, k21a, k21b]
    else:
        early = parts = [lax.all_gather(own, "ctx", axis=0, tiled=True)]
        rc_a = swap(rc_a, "ctx", count - 1)
        rc_b = swap(rc_b, "ctx", count - 1)

    q_near, w_near, coarse, fine = pl.pallas_call(
        prep_kernel,
        name="prep",
        out_shape=(
            pltpu.VMEM(q.shape, bf16),
            pltpu.VMEM(conv_weight.shape, f32),
            pltpu.VMEM((rows, chans), f32),
            pltpu.VMEM((tiles, 2 * rows + 2 * EDGE, LANES), f32),
        ),
        in_specs=[HBM] * 3,
        out_specs=(VMEM,) * 4,
        scratch_shapes=[pltpu.VMEM(f.shape, bf16), pltpu.SemaphoreType.DMA((3,))],
        compiler_params=limit(8),
    )(far(q), far(f), far(conv_weight))

    wide = pl.cdiv(dv, LANES) * LANES
    some = count // 2 * rows
    first = [near(part) for part in early]
    keys_a, lo_a, hi_a, tops, totals, sums = pl.pallas_call(
        lambda *refs: first_kernel(*refs, parts=len(early), per=rows, dv=dv, count=extra),
        name="first",
        out_shape=(
            pltpu.VMEM((some, dk), bf16),
            pltpu.VMEM((wide, some), bf16),
            pltpu.VMEM((wide, some), bf16),
            pltpu.VMEM((HEADS, rows, LANES), f32),
            pltpu.VMEM((HEADS, rows, LANES), f32),
            pltpu.VMEM((HEADS, rows, wide), f32),
        ),
        in_specs=[VMEM] * (1 + len(early)),
        out_specs=(VMEM,) * 6,
        compiler_params=limit(16),
    )(near(q_near), *first)

    base, ends, fine = pl.pallas_call(
        lambda *refs: attend_kernel(*refs, parts=len(parts), per=rows, dv=dv, ring=count == 8),
        name="attend",
        out_shape=(
            pltpu.VMEM((rows, chans), f32),
            pltpu.VMEM((EDGE, chans), f32),
            pltpu.VMEM((tiles, 2 * rows + 2 * EDGE, LANES), f32),
        ),
        in_specs=[VMEM] * (10 + len(parts)),
        out_specs=(VMEM,) * 3,
        scratch_shapes=[
            pltpu.VMEM((some, dk), bf16),
            pltpu.VMEM((wide, some), bf16),
            pltpu.VMEM((wide, some), bf16),
            pltpu.VMEM((count, extra, LANES), f32),
            pltpu.VMEM((EDGE, chans), f32),
        ],
        input_output_aliases={2: 0, 3: 2},
        compiler_params=limit(16),
    )(
        near(q_near),
        near(w_near),
        near(coarse),
        near(fine),
        *[near(x) for x in (keys_a, lo_a, hi_a, tops, totals, sums)],
        *[near(part) for part in parts],
    )

    partial, grad = pl.pallas_call(
        grad_kernel,
        name="grad",
        out_shape=(pltpu.VMEM((KW, chans), f32), pltpu.VMEM((rows, chans), f32)),
        in_specs=[VMEM] * 4,
        out_specs=(VMEM,) * 2,
        compiler_params=limit(8),
    )(near(base), near(fine), near(rc_a), near(rc_b))

    d_fine = pl.pallas_call(
        fine_kernel,
        name="fine",
        out_shape=jax.ShapeDtypeStruct((2 * rows, chans), bf16),
        in_specs=[VMEM] * 3,
        out_specs=VMEM,
        scratch_shapes=[
            pltpu.VMEM((tiles, 2 * rows, LANES), f32),
            pltpu.VMEM((rows + 2 * EDGE, LANES), f32),
        ],
        compiler_params=limit(8),
    )(near(grad), near(ends), near(w_near))

    total = partial
    if count == 8:
        rounds = [("dp", (1 << b,)) for b in range(lax.axis_size("dp").bit_length() - 1)]
        rounds += [("ctx", (1, 2, 3)), ("ctx", (4,))]
    else:
        rounds = [(a, (1 << b,)) for a in ("dp", "ctx") for b in range(lax.axis_size(a).bit_length() - 1)]
    for axis, masks in rounds:
        got = [swap(total, axis, mask) for mask in masks]
        total = sum(got, total)
    scale = 1.0 / math.sqrt(lax.axis_size("dp") * rows * count)
    return (d_fine[None], total * scale)


def solution(mesh):
    placed = (
        P("dp", "ctx", None),
        P("dp", "ctx", None),
        P("dp", "ctx", None),
        P("dp", "ctx", None),
        P("dp", "ctx", None),
        P(),
    )

    return jax.shard_map(body, mesh=mesh, in_specs=placed, out_specs=(P("dp", "ctx", None), P()), check_vma=False)
```

```python
import math

import jax
import jax.numpy as jnp
from jax import lax
from jax.experimental import pallas as pl
from jax.experimental.pallas import tpu as pltpu
from jax.sharding import PartitionSpec as P


HEADS = 8
KW = 5
EDGE = 8
LANES = 128
TAIL = 4
HEAD = 3
TILE = 16
CUT = 7
VMEM = pl.BlockSpec(memory_space=pltpu.VMEM)
HBM = pl.BlockSpec(memory_space=pltpu.HBM)
SMEM = pl.BlockSpec(memory_space=pltpu.SMEM)


def edge_rows(tiles, heads):
    at = {}
    start = 0
    for name, count in (
        ("f_tail", TAIL * tiles),
        ("f_head", HEAD * tiles),
        ("rc_first", tiles),
        ("rc_last", tiles),
        ("q_first", heads),
        ("q_last", heads),
    ):
        at[name] = start
        start += count
    return at, pl.cdiv(start, TILE) * TILE


def pack_kernel(k, vt, q, f, rc, own, rc_a, rc_b, q_ends, f_ends, rc_ends, edges, sem):
    dk, dv = k.shape[0], vt.shape[0]
    half = rc_a.shape[0]
    q_rows, f_rows, rc_rows = q.shape[0], f.shape[0], rc.shape[0]
    copies = [
        (rc.at[0:TILE], rc_ends.at[0:TILE]),
        (rc.at[rc_rows - TILE :], rc_ends.at[TILE:]),
        (q.at[0:TILE], q_ends.at[0:TILE]),
        (q.at[q_rows - TILE :], q_ends.at[TILE:]),
        (f.at[0:TILE], f_ends.at[0:TILE]),
        (f.at[f_rows - TILE :], f_ends.at[TILE:]),
        (k, own.at[0:dk]),
        (vt, own.at[dk : dk + dv]),
        (rc.at[0:half], rc_a),
        (rc.at[half:], rc_b),
    ]
    started = [pltpu.make_async_copy(src, dst, sem.at[i]) for i, (src, dst) in enumerate(copies)]
    for copy in started:
        copy.start()
    for copy in started[:6]:
        copy.wait()
    tiles = rc.shape[1] // LANES
    heads = q.shape[1] // LANES
    at, _ = edge_rows(tiles, heads)
    rc_f = rc_ends[...].astype(jnp.float32)
    q_f = q_ends[...].astype(jnp.float32)
    f_f = f_ends[...].astype(jnp.float32)
    edges[...] = jnp.zeros(edges.shape, jnp.float32)
    for c in range(tiles):
        to = slice(c * LANES, (c + 1) * LANES)
        for j in range(TAIL):
            edges[at["f_tail"] + j * tiles + c] = f_f[2 * TILE - TAIL + j, to]
        for j in range(HEAD):
            edges[at["f_head"] + j * tiles + c] = f_f[j, to]
        edges[at["rc_first"] + c] = rc_f[0, to]
        edges[at["rc_last"] + c] = rc_f[2 * TILE - 1, to]
    for h in range(heads):
        to = slice(h * LANES, (h + 1) * LANES)
        edges[at["q_first"] + h] = q_f[0, to]
        edges[at["q_last"] + h] = q_f[2 * TILE - 1, to]
    own[dk + dv :] = edges[...].astype(own.dtype)
    for copy in started[6:]:
        copy.wait()


def prep_kernel(q, f, w, q_near, w_near, coarse, fine, f_near, sem):
    started = [
        pltpu.make_async_copy(f, f_near, sem.at[0]),
        pltpu.make_async_copy(w, w_near, sem.at[1]),
        pltpu.make_async_copy(q, q_near, sem.at[2]),
    ]
    for copy in started:
        copy.start()
    for copy in started:
        copy.wait()
    rows = coarse.shape[0]
    for c in range(fine.shape[0]):
        to = slice(c * LANES, (c + 1) * LANES)
        fine[c, 0:EDGE] = jnp.zeros((EDGE, LANES), jnp.float32)
        fine[c, EDGE : EDGE + 2 * rows] = f_near[:, to].astype(jnp.float32)
        fine[c, EDGE + 2 * rows :] = jnp.zeros((EDGE, LANES), jnp.float32)
        acc = w_near[0:1, to] * fine[c, pl.ds(EDGE - 2, rows, stride=2), :]
        for k in range(1, KW):
            acc = acc + w_near[k : k + 1, to] * fine[c, pl.ds(EDGE - 2 + k, rows, stride=2), :]
        coarse[:, to] = acc


def load_blocks(blocks, per, dv, keys, vals_lo, vals_hi):
    wide = vals_lo.shape[0]
    for j, (ref, low) in enumerate(blocks):
        to = slice(j * per, (j + 1) * per)
        keys[to] = ref[low : low + per]
        vals_lo[0:dv, to] = ref[low + per : low + per + dv]
        vals_hi[wide - dv :, to] = ref[low + per : low + per + dv]
    span = len(blocks) * per
    vals_lo[dv:] = jnp.zeros((wide - dv, span), vals_lo.dtype)
    vals_hi[0 : wide - dv] = jnp.zeros((wide - dv, span), vals_hi.dtype)


def times(a, b):
    return lax.dot_general(a, b, (((1,), (1,)), ((), ())), preferred_element_type=jnp.float32)


def first_kernel(q, *rest, parts, per, dv, count):
    refs = rest[:parts]
    keys, vals_lo, vals_hi, tops, totals, sums = rest[parts:]
    dk = q.shape[1] // HEADS
    blocks = block_list(refs, per + dv + count)
    load_blocks(blocks[: keys.shape[0] // per], per, dv, keys, vals_lo, vals_hi)
    scale = dk ** (-0.5)
    for h in range(HEADS):
        vals = vals_hi if h % 2 else vals_lo
        s = times(q[:, h * dk : (h + 1) * dk], keys[...]) * scale
        top = jnp.max(s, axis=1, keepdims=True)
        p = jnp.exp(s - top)
        tops[h] = jnp.broadcast_to(top, tops.shape[1:])
        totals[h] = jnp.broadcast_to(jnp.sum(p, axis=1, keepdims=True), totals.shape[1:])
        sums[h] = times(p.astype(jnp.bfloat16), vals[...])


def block_list(refs, size):
    return [(ref, low) for ref in refs for low in range(0, ref.shape[0], size)]


def attend_kernel(q, w, coarse, fine_in, keys_a, lo_a, hi_a, tops, totals, sums, *rest, parts, per, dv, ring):
    refs = rest[:parts]
    base, ends, fine, keys, vals_lo, vals_hi, edges, att_ends = rest[parts:]
    rows, chans = coarse.shape
    dk = q.shape[1] // HEADS
    wide = vals_lo.shape[0]
    tiles = chans // LANES
    at, count = edge_rows(tiles, HEADS)
    blocks = block_list(refs, per + dv + count)
    total_blocks = len(blocks)
    load_blocks(blocks[total_blocks // 2 :], per, dv, keys, vals_lo, vals_hi)
    for j, (ref, low) in enumerate(blocks):
        edges[j] = ref[low + per + dv : low + per + dv + count].astype(jnp.float32)
    here = lax.axis_index("ctx").astype(jnp.int32)

    def spot(other):
        if not ring:
            return jnp.clip(other, 0, total_blocks - 1)
        mask = (here ^ other) & (total_blocks - 1)
        found = jnp.int32(0)
        for i, of in enumerate((0, 4, 2, 1, 6, 3, 5, 7)):
            found = jnp.where(mask == of, jnp.int32(i), found)
        return found

    keep_left = here > 0
    keep_right = here < total_blocks - 1
    left_at, right_at = spot(here - 1), spot(here + 1)
    rc_left_at, rc_right_at = spot(total_blocks - here), spot(total_blocks - 2 - here)
    scale = dk ** (-0.5)
    over = 2 * wide - 2 * dv

    def head(h):
        vals = vals_hi if h % 2 else vals_lo
        s = times(q[:, h * dk : (h + 1) * dk], keys[...]) * scale
        old = tops[h, :, 0:1]
        top = jnp.maximum(old, jnp.max(s, axis=1, keepdims=True))
        fade = jnp.exp(old - top)
        p = jnp.exp(s - top)
        total = totals[h, :, 0:1] * fade + jnp.sum(p, axis=1, keepdims=True)
        return (sums[h] * fade + times(p.astype(jnp.bfloat16), vals[...])) / total

    def spread(h, lo, hi):
        start = dv * h
        return (
            (start, lo[:, : wide - over]),
            (start + wide - over, lo[:, wide - over :] + hi[:, :over]),
            (start + wide, hi[:, over:]),
        )

    for h in range(0, HEADS, 2):
        for start, piece in spread(h, head(h), head(h + 1)):
            to = slice(start, start + piece.shape[1])
            base[:, to] = coarse[:, to] + piece

    q_edge = jnp.concatenate(
        [
            edges[left_at, at["q_last"] : at["q_last"] + HEADS],
            edges[right_at, at["q_first"] : at["q_first"] + HEADS],
        ],
        axis=0,
    ).astype(q.dtype)
    s_a = times(q_edge, keys_a[...]) * scale
    s_b = times(q_edge, keys[...]) * scale
    top = jnp.maximum(jnp.max(s_a, axis=1, keepdims=True), jnp.max(s_b, axis=1, keepdims=True))
    p_a, p_b = jnp.exp(s_a - top), jnp.exp(s_b - top)
    total = jnp.sum(p_a, axis=1, keepdims=True) + jnp.sum(p_b, axis=1, keepdims=True)
    p_a, p_b = p_a.astype(jnp.bfloat16), p_b.astype(jnp.bfloat16)
    edge_lo = (times(p_a, lo_a[...]) + times(p_b, vals_lo[...])) / total
    edge_hi = (times(p_a, hi_a[...]) + times(p_b, vals_hi[...])) / total
    for side in range(2):
        for h in range(0, HEADS, 2):
            i = side * HEADS + h
            for start, piece in spread(h, edge_lo[i : i + 1], edge_hi[i + 1 : i + 2]):
                att_ends[side : side + 1, start : start + piece.shape[1]] = piece

    last = 2 * rows + EDGE
    for c in range(tiles):
        to = slice(c * LANES, (c + 1) * LANES)
        for i in range(TAIL):
            row = at["f_tail"] + i * tiles + c
            fine[c, EDGE - TAIL + i : EDGE - TAIL + i + 1] = jnp.where(keep_left, edges[left_at, row : row + 1], 0.0)
        for i in range(HEAD):
            row = at["f_head"] + i * tiles + c
            fine[c, last + i : last + i + 1] = jnp.where(keep_right, edges[right_at, row : row + 1], 0.0)
        w_c = [w[k : k + 1, to] for k in range(KW)]
        base[0:1, to] = base[0:1, to] + w_c[0] * fine[c, EDGE - 2 : EDGE - 1] + w_c[1] * fine[c, EDGE - 1 : EDGE]
        base[rows - 1 : rows, to] = base[rows - 1 : rows, to] + w_c[4] * fine[c, last : last + 1]
        row = at["rc_first"] + c
        left = att_ends[0:1, to] - edges[rc_left_at, row : row + 1]
        row = at["rc_last"] + c
        right = att_ends[1:2, to] - edges[rc_right_at, row : row + 1]
        for k in range(KW):
            left = left + w_c[k] * fine[c, EDGE - 4 + k : EDGE - 3 + k]
            right = right + w_c[k] * fine[c, last - 2 + k : last - 1 + k]
        ends[0:1, to] = jnp.where(keep_left, left, 0.0)
        ends[1:2, to] = jnp.where(keep_right, right, 0.0)


def grad_kernel(base, fine, rc_a, rc_b, partial, grad):
    rows = base.shape[0]

    def flip(n):
        i = lax.broadcasted_iota(jnp.int32, (n, n), 0)
        j = lax.broadcasted_iota(jnp.int32, (n, n), 1)
        return (i + j == n - 1).astype(jnp.bfloat16)

    pieces = [(rows - rc_a.shape[0], rc_a, flip(rc_a.shape[0])), (0, rc_b, flip(rc_b.shape[0]))]
    for c in range(fine.shape[0]):
        to = slice(c * LANES, (c + 1) * LANES)
        sums = [None] * KW
        for low, rc, turn in pieces:
            n = rc.shape[0]
            g = base[low : low + n, to] - jnp.dot(turn, rc[:, to], preferred_element_type=jnp.float32)
            grad[low : low + n, to] = g
            for k in range(KW):
                tap = fine[c, pl.ds(EDGE - 2 + k + 2 * low, n, stride=2), :]
                term = jnp.sum((g * tap).reshape(n // 8, 8, LANES), axis=0)
                sums[k] = term if sums[k] is None else sums[k] + term
        for k in range(KW):
            partial[k : k + 1, to] = jnp.sum(sums[k], axis=0, keepdims=True)


def fine_kernel(grad, ends, w, d_fine, wide, padded):
    rows = d_fine.shape[0] // 2
    for c in range(wide.shape[0]):
        to = slice(c * LANES, (c + 1) * LANES)
        here = grad[:, to]
        padded[EDGE : EDGE + rows] = here
        padded[EDGE - 1 : EDGE] = ends[0:1, to]
        padded[EDGE + rows : EDGE + rows + 1] = ends[1:2, to]
        after = padded[EDGE + 1 : EDGE + 1 + rows]
        before = padded[EDGE - 1 : EDGE - 1 + rows]
        wide[c, pl.ds(0, rows, stride=2), :] = w[0:1, to] * after + w[2:3, to] * here + w[4:5, to] * before
        wide[c, pl.ds(1, rows, stride=2), :] = w[1:2, to] * after + w[3:4, to] * here
        d_fine[:, to] = wide[c].astype(d_fine.dtype)


def swap(value, axis, mask):
    return lax.ppermute(value, axis, [(i, i ^ mask) for i in range(lax.axis_size(axis))])


def near(value):
    return pltpu.with_memory_space_constraint(value, pltpu.VMEM)


def far(value):
    return pltpu.with_memory_space_constraint(value, pltpu.HBM)


def limit(mib):
    return pltpu.CompilerParams(vmem_limit_bytes=mib << 20)


def body(queries, keys, values, features_fine, rc_state, conv_weight):
    count = lax.axis_size("ctx")
    q, f, rc = queries[0], features_fine[0], rc_state[0]
    rows, chans = rc.shape
    tiles = chans // LANES
    cut = rows * CUT // 16
    dk, dv = keys.shape[2], values.shape[2]
    _, extra = edge_rows(tiles, HEADS)
    size = rows + dv + extra
    bf16, f32 = jnp.bfloat16, jnp.float32

    own, rc_a, rc_b = pl.pallas_call(
        pack_kernel,
        name="pack",
        out_shape=(pltpu.VMEM((size, LANES), bf16), pltpu.VMEM((cut, chans), bf16), pltpu.VMEM((rows - cut, chans), bf16)),
        in_specs=[HBM] * 5,
        out_specs=(VMEM, VMEM, VMEM),
        scratch_shapes=[
            pltpu.VMEM((2 * TILE, q.shape[1]), bf16),
            pltpu.VMEM((2 * TILE, chans), bf16),
            pltpu.VMEM((2 * TILE, chans), bf16),
            pltpu.VMEM((extra, LANES), f32),
            pltpu.SemaphoreType.DMA((10,)),
        ],
        compiler_params=limit(4),
    )(far(keys[0]), far(values[0].T), far(q), far(f), far(rc))

    if count == 8:
        k4 = swap(own, "ctx", 4)
        k2a = swap(own, "ctx", 2)
        k1a = swap(own, "ctx", 1)
        rc_b = swap(rc_b, "ctx", 1)
        rc_a = swap(rc_a, "ctx", 6)
        k2b = swap(k4, "ctx", 2)
        k21a = swap(k2a, "ctx", 1)
        k1b = swap(k4, "ctx", 1)
        rc_b = swap(rc_b, "ctx", 6)
        k21b = swap(k2b, "ctx", 1)
        rc_a = swap(rc_a, "ctx", 1)
        early = [own, k4, k2a, k1a]
        parts = early + [k2b, k21a, k1b, k21b]
    else:
        early = parts = [lax.all_gather(own, "ctx", axis=0, tiled=True)]
        rc_a = swap(rc_a, "ctx", count - 1)
        rc_b = swap(rc_b, "ctx", count - 1)

    q_near, w_near, coarse, fine = pl.pallas_call(
        prep_kernel,
        name="prep",
        out_shape=(
            pltpu.VMEM(q.shape, bf16),
            pltpu.VMEM(conv_weight.shape, f32),
            pltpu.VMEM((rows, chans), f32),
            pltpu.VMEM((tiles, 2 * rows + 2 * EDGE, LANES), f32),
        ),
        in_specs=[HBM] * 3,
        out_specs=(VMEM,) * 4,
        scratch_shapes=[pltpu.VMEM(f.shape, bf16), pltpu.SemaphoreType.DMA((3,))],
        compiler_params=limit(8),
    )(far(q), far(f), far(conv_weight))

    wide = pl.cdiv(dv, LANES) * LANES
    some = count // 2 * rows
    first = [near(part) for part in early]
    keys_a, lo_a, hi_a, tops, totals, sums = pl.pallas_call(
        lambda *refs: first_kernel(*refs, parts=len(early), per=rows, dv=dv, count=extra),
        name="first",
        out_shape=(
            pltpu.VMEM((some, dk), bf16),
            pltpu.VMEM((wide, some), bf16),
            pltpu.VMEM((wide, some), bf16),
            pltpu.VMEM((HEADS, rows, LANES), f32),
            pltpu.VMEM((HEADS, rows, LANES), f32),
            pltpu.VMEM((HEADS, rows, wide), f32),
        ),
        in_specs=[VMEM] * (1 + len(early)),
        out_specs=(VMEM,) * 6,
        compiler_params=limit(16),
    )(near(q_near), *first)

    base, ends, fine = pl.pallas_call(
        lambda *refs: attend_kernel(*refs, parts=len(parts), per=rows, dv=dv, ring=count == 8),
        name="attend",
        out_shape=(
            pltpu.VMEM((rows, chans), f32),
            pltpu.VMEM((EDGE, chans), f32),
            pltpu.VMEM((tiles, 2 * rows + 2 * EDGE, LANES), f32),
        ),
        in_specs=[VMEM] * (10 + len(parts)),
        out_specs=(VMEM,) * 3,
        scratch_shapes=[
            pltpu.VMEM((some, dk), bf16),
            pltpu.VMEM((wide, some), bf16),
            pltpu.VMEM((wide, some), bf16),
            pltpu.VMEM((count, extra, LANES), f32),
            pltpu.VMEM((EDGE, chans), f32),
        ],
        input_output_aliases={2: 0, 3: 2},
        compiler_params=limit(16),
    )(
        near(q_near),
        near(w_near),
        near(coarse),
        near(fine),
        *[near(x) for x in (keys_a, lo_a, hi_a, tops, totals, sums)],
        *[near(part) for part in parts],
    )

    partial, grad = pl.pallas_call(
        grad_kernel,
        name="grad",
        out_shape=(pltpu.VMEM((KW, chans), f32), pltpu.VMEM((rows, chans), f32)),
        in_specs=[VMEM] * 4,
        out_specs=(VMEM,) * 2,
        compiler_params=limit(8),
    )(near(base), near(fine), near(rc_a), near(rc_b))

    d_fine = pl.pallas_call(
        fine_kernel,
        name="fine",
        out_shape=jax.ShapeDtypeStruct((2 * rows, chans), bf16),
        in_specs=[VMEM] * 3,
        out_specs=VMEM,
        scratch_shapes=[
            pltpu.VMEM((tiles, 2 * rows, LANES), f32),
            pltpu.VMEM((rows + 2 * EDGE, LANES), f32),
        ],
        compiler_params=limit(8),
    )(near(grad), near(ends), near(w_near))

    total = partial
    if count == 8 and lax.axis_size("dp") == 4:
        rounds = ((8,), (16, 1, 17), (2, 4, 6))
    else:
        rounds = [(1 << b,) for b in range((lax.axis_size("dp") * count).bit_length() - 1)]
    for masks in rounds:
        got = [swap(total, ("dp", "ctx"), mask) for mask in masks]
        total = sum(got, total)
    scale = 1.0 / math.sqrt(lax.axis_size("dp") * rows * count)
    return (d_fine[None], total * scale)


def solution(mesh):
    placed = (
        P("dp", "ctx", None),
        P("dp", "ctx", None),
        P("dp", "ctx", None),
        P("dp", "ctx", None),
        P("dp", "ctx", None),
        P(),
    )

    return jax.shard_map(
        body, mesh=mesh, in_specs=placed, out_specs=(P("dp", "ctx", None), P()), check_vma=False
    )
```

```python
import math

import jax
import jax.numpy as jnp
from jax import lax
from jax.experimental import pallas as pl
from jax.experimental.pallas import tpu as pltpu
from jax.sharding import PartitionSpec as P


HEADS = 8
KW = 5
EDGE = 8
LANES = 128
TAIL = 4
HEAD = 3
TILE = 16
CUT = 8
VMEM = pl.BlockSpec(memory_space=pltpu.VMEM)
HBM = pl.BlockSpec(memory_space=pltpu.HBM)
SMEM = pl.BlockSpec(memory_space=pltpu.SMEM)


def edge_rows(tiles, heads):
    at = {}
    start = 0
    for name, count in (
        ("f_tail", TAIL * tiles),
        ("f_head", HEAD * tiles),
        ("rc_first", tiles),
        ("rc_last", tiles),
        ("q_first", heads),
        ("q_last", heads),
    ):
        at[name] = start
        start += count
    return at, pl.cdiv(start, TILE) * TILE


def pack_kernel(k, vt, q, f, rc, own, rc_a, rc_b, q_ends, f_ends, rc_ends, edges, sem):
    dk, dv = k.shape[0], vt.shape[0]
    half = rc_a.shape[0]
    q_rows, f_rows, rc_rows = q.shape[0], f.shape[0], rc.shape[0]
    copies = [
        (rc.at[0:TILE], rc_ends.at[0:TILE]),
        (rc.at[rc_rows - TILE :], rc_ends.at[TILE:]),
        (q.at[0:TILE], q_ends.at[0:TILE]),
        (q.at[q_rows - TILE :], q_ends.at[TILE:]),
        (f.at[0:TILE], f_ends.at[0:TILE]),
        (f.at[f_rows - TILE :], f_ends.at[TILE:]),
        (k, own.at[0:dk]),
        (vt, own.at[dk : dk + dv]),
        (rc.at[0:half], rc_a),
        (rc.at[half:], rc_b),
    ]
    started = [pltpu.make_async_copy(src, dst, sem.at[i]) for i, (src, dst) in enumerate(copies)]
    for copy in started:
        copy.start()
    for copy in started[:6]:
        copy.wait()
    tiles = rc.shape[1] // LANES
    heads = q.shape[1] // LANES
    at, _ = edge_rows(tiles, heads)
    rc_f = rc_ends[...].astype(jnp.float32)
    q_f = q_ends[...].astype(jnp.float32)
    f_f = f_ends[...].astype(jnp.float32)
    edges[...] = jnp.zeros(edges.shape, jnp.float32)
    for c in range(tiles):
        to = slice(c * LANES, (c + 1) * LANES)
        for j in range(TAIL):
            edges[at["f_tail"] + j * tiles + c] = f_f[2 * TILE - TAIL + j, to]
        for j in range(HEAD):
            edges[at["f_head"] + j * tiles + c] = f_f[j, to]
        edges[at["rc_first"] + c] = rc_f[0, to]
        edges[at["rc_last"] + c] = rc_f[2 * TILE - 1, to]
    for h in range(heads):
        to = slice(h * LANES, (h + 1) * LANES)
        edges[at["q_first"] + h] = q_f[0, to]
        edges[at["q_last"] + h] = q_f[2 * TILE - 1, to]
    own[dk + dv :] = edges[...].astype(own.dtype)
    for copy in started[6:]:
        copy.wait()


def prep_kernel(q, f, w, q_near, w_near, coarse, fine, f_near, sem):
    started = [
        pltpu.make_async_copy(f, f_near, sem.at[0]),
        pltpu.make_async_copy(w, w_near, sem.at[1]),
        pltpu.make_async_copy(q, q_near, sem.at[2]),
    ]
    for copy in started:
        copy.start()
    for copy in started:
        copy.wait()
    rows = coarse.shape[0]
    for c in range(fine.shape[0]):
        to = slice(c * LANES, (c + 1) * LANES)
        fine[c, 0:EDGE] = jnp.zeros((EDGE, LANES), jnp.float32)
        fine[c, EDGE : EDGE + 2 * rows] = f_near[:, to].astype(jnp.float32)
        fine[c, EDGE + 2 * rows :] = jnp.zeros((EDGE, LANES), jnp.float32)
        acc = w_near[0:1, to] * fine[c, pl.ds(EDGE - 2, rows, stride=2), :]
        for k in range(1, KW):
            acc = acc + w_near[k : k + 1, to] * fine[c, pl.ds(EDGE - 2 + k, rows, stride=2), :]
        coarse[:, to] = acc


def load_blocks(blocks, per, dv, keys, vals_lo, vals_hi):
    wide = vals_lo.shape[0]
    for j, (ref, low) in enumerate(blocks):
        to = slice(j * per, (j + 1) * per)
        keys[to] = ref[low : low + per]
        vals_lo[0:dv, to] = ref[low + per : low + per + dv]
        vals_hi[wide - dv :, to] = ref[low + per : low + per + dv]
    span = len(blocks) * per
    vals_lo[dv:] = jnp.zeros((wide - dv, span), vals_lo.dtype)
    vals_hi[0 : wide - dv] = jnp.zeros((wide - dv, span), vals_hi.dtype)


def times(a, b):
    return lax.dot_general(a, b, (((1,), (1,)), ((), ())), preferred_element_type=jnp.float32)


def first_kernel(q, *rest, parts, per, dv, count):
    refs = rest[:parts]
    keys, vals_lo, vals_hi, tops, totals, sums = rest[parts:]
    dk = q.shape[1] // HEADS
    blocks = block_list(refs, per + dv + count)
    load_blocks(blocks[: keys.shape[0] // per], per, dv, keys, vals_lo, vals_hi)
    scale = dk ** (-0.5)
    for h in range(HEADS):
        vals = vals_hi if h % 2 else vals_lo
        s = times(q[:, h * dk : (h + 1) * dk], keys[...]) * scale
        top = jnp.max(s, axis=1, keepdims=True)
        p = jnp.exp(s - top)
        tops[h] = jnp.broadcast_to(top, tops.shape[1:])
        totals[h] = jnp.broadcast_to(jnp.sum(p, axis=1, keepdims=True), totals.shape[1:])
        sums[h] = times(p.astype(jnp.bfloat16), vals[...])


def block_list(refs, size):
    return [(ref, low) for ref in refs for low in range(0, ref.shape[0], size)]


def attend_kernel(q, w, coarse, fine_in, keys_a, lo_a, hi_a, tops, totals, sums, *rest, parts, per, dv, ring):
    refs = rest[:parts]
    base, ends, fine, keys, vals_lo, vals_hi, edges, att_ends = rest[parts:]
    rows, chans = coarse.shape
    dk = q.shape[1] // HEADS
    wide = vals_lo.shape[0]
    tiles = chans // LANES
    at, count = edge_rows(tiles, HEADS)
    blocks = block_list(refs, per + dv + count)
    total_blocks = len(blocks)
    load_blocks(blocks[total_blocks // 2 :], per, dv, keys, vals_lo, vals_hi)
    for j, (ref, low) in enumerate(blocks):
        edges[j] = ref[low + per + dv : low + per + dv + count].astype(jnp.float32)
    here = lax.axis_index("ctx").astype(jnp.int32)

    def spot(other):
        if not ring:
            return jnp.clip(other, 0, total_blocks - 1)
        mask = (here ^ other) & (total_blocks - 1)
        found = jnp.int32(0)
        for i, of in enumerate((0, 4, 2, 1, 6, 3, 5, 7)):
            found = jnp.where(mask == of, jnp.int32(i), found)
        return found

    keep_left = here > 0
    keep_right = here < total_blocks - 1
    left_at, right_at = spot(here - 1), spot(here + 1)
    rc_left_at, rc_right_at = spot(total_blocks - here), spot(total_blocks - 2 - here)
    scale = dk ** (-0.5)
    over = 2 * wide - 2 * dv

    def head(h):
        vals = vals_hi if h % 2 else vals_lo
        s = times(q[:, h * dk : (h + 1) * dk], keys[...]) * scale
        old = tops[h, :, 0:1]
        top = jnp.maximum(old, jnp.max(s, axis=1, keepdims=True))
        fade = jnp.exp(old - top)
        p = jnp.exp(s - top)
        total = totals[h, :, 0:1] * fade + jnp.sum(p, axis=1, keepdims=True)
        return (sums[h] * fade + times(p.astype(jnp.bfloat16), vals[...])) / total

    def spread(h, lo, hi):
        start = dv * h
        return (
            (start, lo[:, : wide - over]),
            (start + wide - over, lo[:, wide - over :] + hi[:, :over]),
            (start + wide, hi[:, over:]),
        )

    for h in range(0, HEADS, 2):
        for start, piece in spread(h, head(h), head(h + 1)):
            to = slice(start, start + piece.shape[1])
            base[:, to] = coarse[:, to] + piece

    q_edge = jnp.concatenate(
        [
            edges[left_at, at["q_last"] : at["q_last"] + HEADS],
            edges[right_at, at["q_first"] : at["q_first"] + HEADS],
        ],
        axis=0,
    ).astype(q.dtype)
    s_a = times(q_edge, keys_a[...]) * scale
    s_b = times(q_edge, keys[...]) * scale
    top = jnp.maximum(jnp.max(s_a, axis=1, keepdims=True), jnp.max(s_b, axis=1, keepdims=True))
    p_a, p_b = jnp.exp(s_a - top), jnp.exp(s_b - top)
    total = jnp.sum(p_a, axis=1, keepdims=True) + jnp.sum(p_b, axis=1, keepdims=True)
    p_a, p_b = p_a.astype(jnp.bfloat16), p_b.astype(jnp.bfloat16)
    edge_lo = (times(p_a, lo_a[...]) + times(p_b, vals_lo[...])) / total
    edge_hi = (times(p_a, hi_a[...]) + times(p_b, vals_hi[...])) / total
    for side in range(2):
        for h in range(0, HEADS, 2):
            i = side * HEADS + h
            for start, piece in spread(h, edge_lo[i : i + 1], edge_hi[i + 1 : i + 2]):
                att_ends[side : side + 1, start : start + piece.shape[1]] = piece

    last = 2 * rows + EDGE
    for c in range(tiles):
        to = slice(c * LANES, (c + 1) * LANES)
        for i in range(TAIL):
            row = at["f_tail"] + i * tiles + c
            fine[c, EDGE - TAIL + i : EDGE - TAIL + i + 1] = jnp.where(keep_left, edges[left_at, row : row + 1], 0.0)
        for i in range(HEAD):
            row = at["f_head"] + i * tiles + c
            fine[c, last + i : last + i + 1] = jnp.where(keep_right, edges[right_at, row : row + 1], 0.0)
        w_c = [w[k : k + 1, to] for k in range(KW)]
        base[0:1, to] = base[0:1, to] + w_c[0] * fine[c, EDGE - 2 : EDGE - 1] + w_c[1] * fine[c, EDGE - 1 : EDGE]
        base[rows - 1 : rows, to] = base[rows - 1 : rows, to] + w_c[4] * fine[c, last : last + 1]
        row = at["rc_first"] + c
        left = att_ends[0:1, to] - edges[rc_left_at, row : row + 1]
        row = at["rc_last"] + c
        right = att_ends[1:2, to] - edges[rc_right_at, row : row + 1]
        for k in range(KW):
            left = left + w_c[k] * fine[c, EDGE - 4 + k : EDGE - 3 + k]
            right = right + w_c[k] * fine[c, last - 2 + k : last - 1 + k]
        ends[0:1, to] = jnp.where(keep_left, left, 0.0)
        ends[1:2, to] = jnp.where(keep_right, right, 0.0)


def grad_kernel(base, fine, rc_a, rc_b, partial, grad):
    rows = base.shape[0]

    def flip(n):
        i = lax.broadcasted_iota(jnp.int32, (n, n), 0)
        j = lax.broadcasted_iota(jnp.int32, (n, n), 1)
        return (i + j == n - 1).astype(jnp.bfloat16)

    pieces = [(rows - rc_a.shape[0], rc_a, flip(rc_a.shape[0])), (0, rc_b, flip(rc_b.shape[0]))]
    for c in range(fine.shape[0]):
        to = slice(c * LANES, (c + 1) * LANES)
        sums = [None] * KW
        for low, rc, turn in pieces:
            n = rc.shape[0]
            g = base[low : low + n, to] - jnp.dot(turn, rc[:, to], preferred_element_type=jnp.float32)
            grad[low : low + n, to] = g
            for k in range(KW):
                tap = fine[c, pl.ds(EDGE - 2 + k + 2 * low, n, stride=2), :]
                term = jnp.sum((g * tap).reshape(n // 8, 8, LANES), axis=0)
                sums[k] = term if sums[k] is None else sums[k] + term
        for k in range(KW):
            partial[k : k + 1, to] = jnp.sum(sums[k], axis=0, keepdims=True)


def fine_kernel(grad, ends, w, d_fine, wide, padded):
    rows = d_fine.shape[0] // 2
    for c in range(wide.shape[0]):
        to = slice(c * LANES, (c + 1) * LANES)
        here = grad[:, to]
        padded[EDGE : EDGE + rows] = here
        padded[EDGE - 1 : EDGE] = ends[0:1, to]
        padded[EDGE + rows : EDGE + rows + 1] = ends[1:2, to]
        after = padded[EDGE + 1 : EDGE + 1 + rows]
        before = padded[EDGE - 1 : EDGE - 1 + rows]
        wide[c, pl.ds(0, rows, stride=2), :] = w[0:1, to] * after + w[2:3, to] * here + w[4:5, to] * before
        wide[c, pl.ds(1, rows, stride=2), :] = w[1:2, to] * after + w[3:4, to] * here
        d_fine[:, to] = wide[c].astype(d_fine.dtype)


def swap(value, axis, mask):
    return lax.ppermute(value, axis, [(i, i ^ mask) for i in range(lax.axis_size(axis))])


def near(value):
    return pltpu.with_memory_space_constraint(value, pltpu.VMEM)


def far(value):
    return pltpu.with_memory_space_constraint(value, pltpu.HBM)


def limit(mib):
    return pltpu.CompilerParams(vmem_limit_bytes=mib << 20)


def body(queries, keys, values, features_fine, rc_state, conv_weight):
    count = lax.axis_size("ctx")
    q, f, rc = queries[0], features_fine[0], rc_state[0]
    rows, chans = rc.shape
    tiles = chans // LANES
    cut = rows * CUT // 16
    dk, dv = keys.shape[2], values.shape[2]
    _, extra = edge_rows(tiles, HEADS)
    size = rows + dv + extra
    bf16, f32 = jnp.bfloat16, jnp.float32

    own, rc_a, rc_b = pl.pallas_call(
        pack_kernel,
        name="pack",
        out_shape=(pltpu.VMEM((size, LANES), bf16), pltpu.VMEM((cut, chans), bf16), pltpu.VMEM((rows - cut, chans), bf16)),
        in_specs=[HBM] * 5,
        out_specs=(VMEM, VMEM, VMEM),
        scratch_shapes=[
            pltpu.VMEM((2 * TILE, q.shape[1]), bf16),
            pltpu.VMEM((2 * TILE, chans), bf16),
            pltpu.VMEM((2 * TILE, chans), bf16),
            pltpu.VMEM((extra, LANES), f32),
            pltpu.SemaphoreType.DMA((10,)),
        ],
        compiler_params=limit(4),
    )(far(keys[0]), far(values[0].T), far(q), far(f), far(rc))

    if count == 8:
        k4 = swap(own, "ctx", 4)
        k2a = swap(own, "ctx", 2)
        k1a = swap(own, "ctx", 1)
        rc_b = swap(rc_b, "ctx", 1)
        rc_a = swap(rc_a, "ctx", 6)
        k2b = swap(k4, "ctx", 2)
        k21a = swap(k2a, "ctx", 1)
        k1b = swap(k4, "ctx", 1)
        rc_b = swap(rc_b, "ctx", 6)
        k21b = swap(k2b, "ctx", 1)
        rc_a = swap(rc_a, "ctx", 1)
        early = [own, k4, k2a, k1a]
        parts = early + [k2b, k21a, k1b, k21b]
    else:
        early = parts = [lax.all_gather(own, "ctx", axis=0, tiled=True)]
        rc_a = swap(rc_a, "ctx", count - 1)
        rc_b = swap(rc_b, "ctx", count - 1)

    q_near, w_near, coarse, fine = pl.pallas_call(
        prep_kernel,
        name="prep",
        out_shape=(
            pltpu.VMEM(q.shape, bf16),
            pltpu.VMEM(conv_weight.shape, f32),
            pltpu.VMEM((rows, chans), f32),
            pltpu.VMEM((tiles, 2 * rows + 2 * EDGE, LANES), f32),
        ),
        in_specs=[HBM] * 3,
        out_specs=(VMEM,) * 4,
        scratch_shapes=[pltpu.VMEM(f.shape, bf16), pltpu.SemaphoreType.DMA((3,))],
        compiler_params=limit(8),
    )(far(q), far(f), far(conv_weight))

    wide = pl.cdiv(dv, LANES) * LANES
    some = count // 2 * rows
    first = [near(part) for part in early]
    keys_a, lo_a, hi_a, tops, totals, sums = pl.pallas_call(
        lambda *refs: first_kernel(*refs, parts=len(early), per=rows, dv=dv, count=extra),
        name="first",
        out_shape=(
            pltpu.VMEM((some, dk), bf16),
            pltpu.VMEM((wide, some), bf16),
            pltpu.VMEM((wide, some), bf16),
            pltpu.VMEM((HEADS, rows, LANES), f32),
            pltpu.VMEM((HEADS, rows, LANES), f32),
            pltpu.VMEM((HEADS, rows, wide), f32),
        ),
        in_specs=[VMEM] * (1 + len(early)),
        out_specs=(VMEM,) * 6,
        compiler_params=limit(16),
    )(near(q_near), *first)

    base, ends, fine = pl.pallas_call(
        lambda *refs: attend_kernel(*refs, parts=len(parts), per=rows, dv=dv, ring=count == 8),
        name="attend",
        out_shape=(
            pltpu.VMEM((rows, chans), f32),
            pltpu.VMEM((EDGE, chans), f32),
            pltpu.VMEM((tiles, 2 * rows + 2 * EDGE, LANES), f32),
        ),
        in_specs=[VMEM] * (10 + len(parts)),
        out_specs=(VMEM,) * 3,
        scratch_shapes=[
            pltpu.VMEM((some, dk), bf16),
            pltpu.VMEM((wide, some), bf16),
            pltpu.VMEM((wide, some), bf16),
            pltpu.VMEM((count, extra, LANES), f32),
            pltpu.VMEM((EDGE, chans), f32),
        ],
        input_output_aliases={2: 0, 3: 2},
        compiler_params=limit(16),
    )(
        near(q_near),
        near(w_near),
        near(coarse),
        near(fine),
        *[near(x) for x in (keys_a, lo_a, hi_a, tops, totals, sums)],
        *[near(part) for part in parts],
    )

    partial, grad = pl.pallas_call(
        grad_kernel,
        name="grad",
        out_shape=(pltpu.VMEM((KW, chans), f32), pltpu.VMEM((rows, chans), f32)),
        in_specs=[VMEM] * 4,
        out_specs=(VMEM,) * 2,
        compiler_params=limit(8),
    )(near(base), near(fine), near(rc_a), near(rc_b))

    d_fine = pl.pallas_call(
        fine_kernel,
        name="fine",
        out_shape=jax.ShapeDtypeStruct((2 * rows, chans), bf16),
        in_specs=[VMEM] * 3,
        out_specs=VMEM,
        scratch_shapes=[
            pltpu.VMEM((tiles, 2 * rows, LANES), f32),
            pltpu.VMEM((rows + 2 * EDGE, LANES), f32),
        ],
        compiler_params=limit(8),
    )(near(grad), near(ends), near(w_near))

    total = partial
    if count == 8 and lax.axis_size("dp") == 4:
        rounds = ((8,), (16, 1, 17), (2, 4, 6))
    else:
        rounds = [(1 << b,) for b in range((lax.axis_size("dp") * count).bit_length() - 1)]
    for masks in rounds:
        got = [swap(total, ("dp", "ctx"), mask) for mask in masks]
        total = sum(got, total)
    scale = 1.0 / math.sqrt(lax.axis_size("dp") * rows * count)
    return (d_fine[None], total * scale)


def solution(mesh):
    placed = (
        P("dp", "ctx", None),
        P("dp", "ctx", None),
        P("dp", "ctx", None),
        P("dp", "ctx", None),
        P("dp", "ctx", None),
        P(),
    )

    return jax.shard_map(body, mesh=mesh, in_specs=placed, out_specs=(P("dp", "ctx", None), P()), check_vma=False)
```

```python
import math

import jax
import jax.numpy as jnp
from jax import lax
from jax.experimental import pallas as pl
from jax.experimental.pallas import tpu as pltpu
from jax.sharding import PartitionSpec as P


HEADS = 8
KW = 5
EDGE = 8
LANES = 128
TAIL = 4
HEAD = 3
TILE = 16
CUT = 8
VMEM = pl.BlockSpec(memory_space=pltpu.VMEM)
HBM = pl.BlockSpec(memory_space=pltpu.HBM)
SMEM = pl.BlockSpec(memory_space=pltpu.SMEM)


def edge_rows(tiles, heads):
    at = {}
    start = 0
    for name, count in (
        ("f_tail", TAIL * tiles),
        ("f_head", HEAD * tiles),
        ("rc_first", tiles),
        ("rc_last", tiles),
        ("q_first", heads),
        ("q_last", heads),
    ):
        at[name] = start
        start += count
    return at, pl.cdiv(start, TILE) * TILE


def pack_kernel(k, vt, q, f, rc, own, rc_a, rc_b, q_ends, f_ends, rc_ends, edges, sem):
    dk, dv = k.shape[0], vt.shape[0]
    half = rc_a.shape[0]
    q_rows, f_rows, rc_rows = q.shape[0], f.shape[0], rc.shape[0]
    copies = [
        (rc.at[0:TILE], rc_ends.at[0:TILE]),
        (rc.at[rc_rows - TILE :], rc_ends.at[TILE:]),
        (q.at[0:TILE], q_ends.at[0:TILE]),
        (q.at[q_rows - TILE :], q_ends.at[TILE:]),
        (f.at[0:TILE], f_ends.at[0:TILE]),
        (f.at[f_rows - TILE :], f_ends.at[TILE:]),
        (k, own.at[0:dk]),
        (vt, own.at[dk : dk + dv]),
        (rc.at[0:half], rc_a),
        (rc.at[half:], rc_b),
    ]
    started = [pltpu.make_async_copy(src, dst, sem.at[i]) for i, (src, dst) in enumerate(copies)]
    for copy in started:
        copy.start()
    for copy in started[:6]:
        copy.wait()
    tiles = rc.shape[1] // LANES
    heads = q.shape[1] // LANES
    at, _ = edge_rows(tiles, heads)
    rc_f = rc_ends[...].astype(jnp.float32)
    q_f = q_ends[...].astype(jnp.float32)
    f_f = f_ends[...].astype(jnp.float32)
    edges[...] = jnp.zeros(edges.shape, jnp.float32)
    for c in range(tiles):
        to = slice(c * LANES, (c + 1) * LANES)
        for j in range(TAIL):
            edges[at["f_tail"] + j * tiles + c] = f_f[2 * TILE - TAIL + j, to]
        for j in range(HEAD):
            edges[at["f_head"] + j * tiles + c] = f_f[j, to]
        edges[at["rc_first"] + c] = rc_f[0, to]
        edges[at["rc_last"] + c] = rc_f[2 * TILE - 1, to]
    for h in range(heads):
        to = slice(h * LANES, (h + 1) * LANES)
        edges[at["q_first"] + h] = q_f[0, to]
        edges[at["q_last"] + h] = q_f[2 * TILE - 1, to]
    own[dk + dv :] = edges[...].astype(own.dtype)
    for copy in started[6:]:
        copy.wait()


def prep_kernel(q, f, w, q_near, w_near, coarse, fine, f_near, sem):
    started = [
        pltpu.make_async_copy(f, f_near, sem.at[0]),
        pltpu.make_async_copy(w, w_near, sem.at[1]),
        pltpu.make_async_copy(q, q_near, sem.at[2]),
    ]
    for copy in started:
        copy.start()
    for copy in started:
        copy.wait()
    rows = coarse.shape[0]
    for c in range(fine.shape[0]):
        to = slice(c * LANES, (c + 1) * LANES)
        fine[c, 0:EDGE] = jnp.zeros((EDGE, LANES), jnp.float32)
        fine[c, EDGE : EDGE + 2 * rows] = f_near[:, to].astype(jnp.float32)
        fine[c, EDGE + 2 * rows :] = jnp.zeros((EDGE, LANES), jnp.float32)
        acc = w_near[0:1, to] * fine[c, pl.ds(EDGE - 2, rows, stride=2), :]
        for k in range(1, KW):
            acc = acc + w_near[k : k + 1, to] * fine[c, pl.ds(EDGE - 2 + k, rows, stride=2), :]
        coarse[:, to] = acc


def load_blocks(blocks, per, dv, keys, vals_lo, vals_hi):
    wide = vals_lo.shape[0]
    for j, (ref, low) in enumerate(blocks):
        to = slice(j * per, (j + 1) * per)
        keys[to] = ref[low : low + per]
        vals_lo[0:dv, to] = ref[low + per : low + per + dv]
        vals_hi[wide - dv :, to] = ref[low + per : low + per + dv]
    span = len(blocks) * per
    vals_lo[dv:] = jnp.zeros((wide - dv, span), vals_lo.dtype)
    vals_hi[0 : wide - dv] = jnp.zeros((wide - dv, span), vals_hi.dtype)


def times(a, b):
    return lax.dot_general(a, b, (((1,), (1,)), ((), ())), preferred_element_type=jnp.float32)


def first_kernel(q, *rest, parts, per, dv, count):
    refs = rest[:parts]
    keys, vals_lo, vals_hi, tops, totals, sums = rest[parts:]
    dk = q.shape[1] // HEADS
    blocks = block_list(refs, per + dv + count)
    load_blocks(blocks[: keys.shape[0] // per], per, dv, keys, vals_lo, vals_hi)
    scale = dk ** (-0.5)
    for h in range(HEADS):
        vals = vals_hi if h % 2 else vals_lo
        s = times(q[:, h * dk : (h + 1) * dk], keys[...]) * scale
        top = jnp.max(s, axis=1, keepdims=True)
        p = jnp.exp(s - top)
        tops[h] = jnp.broadcast_to(top, tops.shape[1:])
        totals[h] = jnp.broadcast_to(jnp.sum(p, axis=1, keepdims=True), totals.shape[1:])
        sums[h] = times(p.astype(jnp.bfloat16), vals[...])


def block_list(refs, size):
    return [(ref, low) for ref in refs for low in range(0, ref.shape[0], size)]


def attend_kernel(q, w, coarse, fine_in, keys_a, lo_a, hi_a, tops, totals, sums, *rest, parts, per, dv, ring):
    refs = rest[:parts]
    base, ends, fine, keys, vals_lo, vals_hi, edges, att_ends = rest[parts:]
    rows, chans = coarse.shape
    dk = q.shape[1] // HEADS
    wide = vals_lo.shape[0]
    tiles = chans // LANES
    at, count = edge_rows(tiles, HEADS)
    blocks = block_list(refs, per + dv + count)
    total_blocks = len(blocks)
    load_blocks(blocks[total_blocks // 2 :], per, dv, keys, vals_lo, vals_hi)
    for j, (ref, low) in enumerate(blocks):
        edges[j] = ref[low + per + dv : low + per + dv + count].astype(jnp.float32)
    here = lax.axis_index("ctx").astype(jnp.int32)

    def spot(other):
        if not ring:
            return jnp.clip(other, 0, total_blocks - 1)
        mask = (here ^ other) & (total_blocks - 1)
        found = jnp.int32(0)
        for i, of in enumerate((0, 4, 2, 1, 6, 3, 5, 7)):
            found = jnp.where(mask == of, jnp.int32(i), found)
        return found

    keep_left = here > 0
    keep_right = here < total_blocks - 1
    left_at, right_at = spot(here - 1), spot(here + 1)
    rc_left_at, rc_right_at = spot(total_blocks - here), spot(total_blocks - 2 - here)
    scale = dk ** (-0.5)
    over = 2 * wide - 2 * dv

    def head(h):
        vals = vals_hi if h % 2 else vals_lo
        s = times(q[:, h * dk : (h + 1) * dk], keys[...]) * scale
        old = tops[h, :, 0:1]
        top = jnp.maximum(old, jnp.max(s, axis=1, keepdims=True))
        fade = jnp.exp(old - top)
        p = jnp.exp(s - top)
        total = totals[h, :, 0:1] * fade + jnp.sum(p, axis=1, keepdims=True)
        return (sums[h] * fade + times(p.astype(jnp.bfloat16), vals[...])) / total

    def spread(h, lo, hi):
        start = dv * h
        return (
            (start, lo[:, : wide - over]),
            (start + wide - over, lo[:, wide - over :] + hi[:, :over]),
            (start + wide, hi[:, over:]),
        )

    for h in range(0, HEADS, 2):
        for start, piece in spread(h, head(h), head(h + 1)):
            to = slice(start, start + piece.shape[1])
            base[:, to] = coarse[:, to] + piece

    q_edge = jnp.concatenate(
        [
            edges[left_at, at["q_last"] : at["q_last"] + HEADS],
            edges[right_at, at["q_first"] : at["q_first"] + HEADS],
        ],
        axis=0,
    ).astype(q.dtype)
    s_a = times(q_edge, keys_a[...]) * scale
    s_b = times(q_edge, keys[...]) * scale
    top = jnp.maximum(jnp.max(s_a, axis=1, keepdims=True), jnp.max(s_b, axis=1, keepdims=True))
    p_a, p_b = jnp.exp(s_a - top), jnp.exp(s_b - top)
    total = jnp.sum(p_a, axis=1, keepdims=True) + jnp.sum(p_b, axis=1, keepdims=True)
    p_a, p_b = p_a.astype(jnp.bfloat16), p_b.astype(jnp.bfloat16)
    edge_lo = (times(p_a, lo_a[...]) + times(p_b, vals_lo[...])) / total
    edge_hi = (times(p_a, hi_a[...]) + times(p_b, vals_hi[...])) / total
    for side in range(2):
        for h in range(0, HEADS, 2):
            i = side * HEADS + h
            for start, piece in spread(h, edge_lo[i : i + 1], edge_hi[i + 1 : i + 2]):
                att_ends[side : side + 1, start : start + piece.shape[1]] = piece

    last = 2 * rows + EDGE
    for c in range(tiles):
        to = slice(c * LANES, (c + 1) * LANES)
        for i in range(TAIL):
            row = at["f_tail"] + i * tiles + c
            fine[c, EDGE - TAIL + i : EDGE - TAIL + i + 1] = jnp.where(keep_left, edges[left_at, row : row + 1], 0.0)
        for i in range(HEAD):
            row = at["f_head"] + i * tiles + c
            fine[c, last + i : last + i + 1] = jnp.where(keep_right, edges[right_at, row : row + 1], 0.0)
        w_c = [w[k : k + 1, to] for k in range(KW)]
        base[0:1, to] = base[0:1, to] + w_c[0] * fine[c, EDGE - 2 : EDGE - 1] + w_c[1] * fine[c, EDGE - 1 : EDGE]
        base[rows - 1 : rows, to] = base[rows - 1 : rows, to] + w_c[4] * fine[c, last : last + 1]
        row = at["rc_first"] + c
        left = att_ends[0:1, to] - edges[rc_left_at, row : row + 1]
        row = at["rc_last"] + c
        right = att_ends[1:2, to] - edges[rc_right_at, row : row + 1]
        for k in range(KW):
            left = left + w_c[k] * fine[c, EDGE - 4 + k : EDGE - 3 + k]
            right = right + w_c[k] * fine[c, last - 2 + k : last - 1 + k]
        ends[0:1, to] = jnp.where(keep_left, left, 0.0)
        ends[1:2, to] = jnp.where(keep_right, right, 0.0)


def grad_kernel(base, fine, rc, *rest, low, chain):
    partial, grad = rest[-2:]
    n = rc.shape[0]
    i = lax.broadcasted_iota(jnp.int32, (n, n), 0)
    j = lax.broadcasted_iota(jnp.int32, (n, n), 1)
    turn = (i + j == n - 1).astype(jnp.bfloat16)
    for c in range(fine.shape[0]):
        to = slice(c * LANES, (c + 1) * LANES)
        g = base[low : low + n, to] - jnp.dot(turn, rc[:, to], preferred_element_type=jnp.float32)
        grad[:, to] = g
        for k in range(KW):
            tap = fine[c, pl.ds(EDGE - 2 + k + 2 * low, n, stride=2), :]
            total = jnp.sum((g * tap).reshape(n // 8, 8, LANES), axis=0)
            total = jnp.sum(total, axis=0, keepdims=True)
            if chain:
                total = total + rest[0][k : k + 1, to]
            partial[k : k + 1, to] = total


def fine_kernel(grad_b, grad_a, ends, w, d_fine, wide, padded):
    rows = d_fine.shape[0] // 2
    for c in range(wide.shape[0]):
        to = slice(c * LANES, (c + 1) * LANES)
        low = grad_b.shape[0]
        padded[EDGE : EDGE + low] = grad_b[:, to]
        padded[EDGE + low : EDGE + rows] = grad_a[:, to]
        here = padded[EDGE : EDGE + rows]
        padded[EDGE - 1 : EDGE] = ends[0:1, to]
        padded[EDGE + rows : EDGE + rows + 1] = ends[1:2, to]
        after = padded[EDGE + 1 : EDGE + 1 + rows]
        before = padded[EDGE - 1 : EDGE - 1 + rows]
        wide[c, pl.ds(0, rows, stride=2), :] = w[0:1, to] * after + w[2:3, to] * here + w[4:5, to] * before
        wide[c, pl.ds(1, rows, stride=2), :] = w[1:2, to] * after + w[3:4, to] * here
        d_fine[:, to] = wide[c].astype(d_fine.dtype)


def swap(value, axis, mask):
    return lax.ppermute(value, axis, [(i, i ^ mask) for i in range(lax.axis_size(axis))])


def near(value):
    return pltpu.with_memory_space_constraint(value, pltpu.VMEM)


def far(value):
    return pltpu.with_memory_space_constraint(value, pltpu.HBM)


def limit(mib):
    return pltpu.CompilerParams(vmem_limit_bytes=mib << 20)


def body(queries, keys, values, features_fine, rc_state, conv_weight):
    count = lax.axis_size("ctx")
    q, f, rc = queries[0], features_fine[0], rc_state[0]
    rows, chans = rc.shape
    tiles = chans // LANES
    cut = rows * CUT // 16
    dk, dv = keys.shape[2], values.shape[2]
    _, extra = edge_rows(tiles, HEADS)
    size = rows + dv + extra
    bf16, f32 = jnp.bfloat16, jnp.float32

    own, rc_a, rc_b = pl.pallas_call(
        pack_kernel,
        name="pack",
        out_shape=(pltpu.VMEM((size, LANES), bf16), pltpu.VMEM((cut, chans), bf16), pltpu.VMEM((rows - cut, chans), bf16)),
        in_specs=[HBM] * 5,
        out_specs=(VMEM, VMEM, VMEM),
        scratch_shapes=[
            pltpu.VMEM((2 * TILE, q.shape[1]), bf16),
            pltpu.VMEM((2 * TILE, chans), bf16),
            pltpu.VMEM((2 * TILE, chans), bf16),
            pltpu.VMEM((extra, LANES), f32),
            pltpu.SemaphoreType.DMA((10,)),
        ],
        compiler_params=limit(4),
    )(far(keys[0]), far(values[0].T), far(q), far(f), far(rc))

    if count == 8:
        k4 = swap(own, "ctx", 4)
        k2a = swap(own, "ctx", 2)
        k1a = swap(own, "ctx", 1)
        rc_b = swap(rc_b, "ctx", 1)
        rc_a = swap(rc_a, "ctx", 6)
        k2b = swap(k4, "ctx", 2)
        k21a = swap(k2a, "ctx", 1)
        k1b = swap(k4, "ctx", 1)
        rc_b = swap(rc_b, "ctx", 6)
        k21b = swap(k2b, "ctx", 1)
        rc_a = swap(rc_a, "ctx", 1)
        early = [own, k4, k2a, k1a]
        parts = early + [k2b, k21a, k1b, k21b]
    else:
        early = parts = [lax.all_gather(own, "ctx", axis=0, tiled=True)]
        rc_a = swap(rc_a, "ctx", count - 1)
        rc_b = swap(rc_b, "ctx", count - 1)

    q_near, w_near, coarse, fine = pl.pallas_call(
        prep_kernel,
        name="prep",
        out_shape=(
            pltpu.VMEM(q.shape, bf16),
            pltpu.VMEM(conv_weight.shape, f32),
            pltpu.VMEM((rows, chans), f32),
            pltpu.VMEM((tiles, 2 * rows + 2 * EDGE, LANES), f32),
        ),
        in_specs=[HBM] * 3,
        out_specs=(VMEM,) * 4,
        scratch_shapes=[pltpu.VMEM(f.shape, bf16), pltpu.SemaphoreType.DMA((3,))],
        compiler_params=limit(8),
    )(far(q), far(f), far(conv_weight))

    wide = pl.cdiv(dv, LANES) * LANES
    some = count // 2 * rows
    first = [near(part) for part in early]
    keys_a, lo_a, hi_a, tops, totals, sums = pl.pallas_call(
        lambda *refs: first_kernel(*refs, parts=len(early), per=rows, dv=dv, count=extra),
        name="first",
        out_shape=(
            pltpu.VMEM((some, dk), bf16),
            pltpu.VMEM((wide, some), bf16),
            pltpu.VMEM((wide, some), bf16),
            pltpu.VMEM((HEADS, rows, LANES), f32),
            pltpu.VMEM((HEADS, rows, LANES), f32),
            pltpu.VMEM((HEADS, rows, wide), f32),
        ),
        in_specs=[VMEM] * (1 + len(early)),
        out_specs=(VMEM,) * 6,
        compiler_params=limit(16),
    )(near(q_near), *first)

    base, ends, fine = pl.pallas_call(
        lambda *refs: attend_kernel(*refs, parts=len(parts), per=rows, dv=dv, ring=count == 8),
        name="attend",
        out_shape=(
            pltpu.VMEM((rows, chans), f32),
            pltpu.VMEM((EDGE, chans), f32),
            pltpu.VMEM((tiles, 2 * rows + 2 * EDGE, LANES), f32),
        ),
        in_specs=[VMEM] * (10 + len(parts)),
        out_specs=(VMEM,) * 3,
        scratch_shapes=[
            pltpu.VMEM((some, dk), bf16),
            pltpu.VMEM((wide, some), bf16),
            pltpu.VMEM((wide, some), bf16),
            pltpu.VMEM((count, extra, LANES), f32),
            pltpu.VMEM((EDGE, chans), f32),
        ],
        input_output_aliases={2: 0, 3: 2},
        compiler_params=limit(16),
    )(
        near(q_near),
        near(w_near),
        near(coarse),
        near(fine),
        *[near(x) for x in (keys_a, lo_a, hi_a, tops, totals, sums)],
        *[near(part) for part in parts],
    )

    half_grads = []
    partial = None
    for low, rc in ((rows - rc_a.shape[0], rc_a), (0, rc_b)):
        have = [] if partial is None else [near(partial)]
        partial, part_grad = pl.pallas_call(
            lambda *refs, low=low, chain=bool(have): grad_kernel(*refs, low=low, chain=chain),
            out_shape=(pltpu.VMEM((KW, chans), f32), pltpu.VMEM((rc.shape[0], chans), f32)),
            in_specs=[VMEM] * (3 + len(have)),
            out_specs=(VMEM,) * 2,
            compiler_params=limit(8),
        )(near(base), near(fine), near(rc), *have)
        half_grads.append(near(part_grad))

    d_fine = pl.pallas_call(
        fine_kernel,
        name="fine",
        out_shape=jax.ShapeDtypeStruct((2 * rows, chans), bf16),
        in_specs=[VMEM] * 4,
        out_specs=VMEM,
        scratch_shapes=[
            pltpu.VMEM((tiles, 2 * rows, LANES), f32),
            pltpu.VMEM((rows + 2 * EDGE, LANES), f32),
        ],
        compiler_params=limit(8),
    )(*half_grads[::-1], near(ends), near(w_near))

    total = partial
    if count == 8 and lax.axis_size("dp") == 4:
        rounds = ((8,), (16, 1, 17), (2, 4, 6))
    else:
        rounds = [(1 << b,) for b in range((lax.axis_size("dp") * count).bit_length() - 1)]
    for masks in rounds:
        got = [swap(total, ("dp", "ctx"), mask) for mask in masks]
        total = sum(got, total)
    scale = 1.0 / math.sqrt(lax.axis_size("dp") * rows * count)
    return (d_fine[None], total * scale)


def solution(mesh):
    placed = (
        P("dp", "ctx", None),
        P("dp", "ctx", None),
        P("dp", "ctx", None),
        P("dp", "ctx", None),
        P("dp", "ctx", None),
        P(),
    )

    return jax.shard_map(
        body, mesh=mesh, in_specs=placed, out_specs=(P("dp", "ctx", None), P()), check_vma=False
    )
```
